32 devices in a mesh: fsdp: 4 (over x, core), ctx: 4 (over z), tp: 2 (over y).
Axes of the slice: x: 2, y: 2, z: 4, core: 2. Of those that a mesh axis runs over, the one named last changes fastest.
Arguments:
- tokens: bfloat16 [8, 4096, 768], P('fsdp', 'ctx'), may hold values from -6 to 6
- qkv_weight: bfloat16 [768, 3, 768], P(('fsdp', 'ctx'), None, 'tp'), may hold values from -0.21875 to 0.21875
- qv_bias: bfloat16 [2, 768], P(None, 'tp'), may hold values from -3 to 3
- out_weight: bfloat16 [768, 768], P(('fsdp', 'ctx'), 'tp'), may hold values from -8 to 8
- up_weight: bfloat16 [768, 3072], P(('fsdp', 'ctx'), 'tp'), may hold values from -0.21875 to 0.21875
- up_bias: bfloat16 [3072], P('tp'), may hold values from -3 to 3
- down_weight: bfloat16 [768, 3072], P(('fsdp', 'ctx'), 'tp'), may hold values from -0.109375 to 0.109375
- norm_gains: bfloat16 [768, 2], P(('fsdp', 'ctx')), may hold values from 0.5 to 1.5
- row_biases: bfloat16 [768, 4], P(('fsdp', 'ctx')), may hold values from -3 to 3
- cotangent: bfloat16 [8, 4096, 768], P('fsdp', 'ctx'), may hold values from -6 to 6
Outputs:
- output: bfloat16 [8, 4096, 768], P('fsdp', ('ctx', 'tp'))
- tokens_grad: bfloat16 [8, 4096, 768], P('fsdp', ('ctx', 'tp'))
- qkv_weight_grad: float32 [768, 3, 768], P(('fsdp', 'ctx'), None, 'tp')
- qv_bias_grad: float32 [2, 768], P(None, 'tp')
- out_weight_grad: float32 [768, 768], P(('fsdp', 'ctx'), 'tp')
- up_weight_grad: float32 [768, 3072], P(('fsdp', 'ctx'), 'tp')
- up_bias_grad: float32 [3072], P('tp')
- down_weight_grad: float32 [768, 3072], P(('fsdp', 'ctx'), 'tp')
- norm_gains_grad: float32 [768, 2], P(('fsdp', 'ctx'))
- row_biases_grad: float32 [768, 4], P(('fsdp', 'ctx'))
The draws below stay inside these ranges and needn't reach their ends.
All inputs are finite; a program needn't handle non-finite values.
Results may differ from the reference program's by a relative error of at most 0.02.
Values may be sent and summed in bfloat16 or wider, within the bound.
No kernel may reach another device: no remote copies, remote signals or barrier semaphores. Data moves between devices by JAX's collectives and lax.ppermute only.
A program may use at most 256 MiB of HBM per device.

```python
import jax
import jax.numpy as jnp
from jax import lax

D = 768
H = 12
HD = 64
FF = 3072
LENGTH = 4096
SEQS = 8


def level_of(own_key, dims, cuts, low, high):
    def one(position, blocks):
        draws = jax.random.uniform(jax.random.fold_in(jax.random.fold_in(own_key, 6), position), (blocks,), jnp.float32, low / len(cuts), high / len(cuts))
        return jnp.repeat(jnp.exp(draws), dims[position] // blocks).reshape((-1,) + (1,) * (len(dims) - position - 1))

    level = one(*cuts[0])
    for cut in cuts[1:]:
        level = level * one(*cut)
    return level


def centred(stream_key, shape, spread, reach, shards=(), kind=jnp.bfloat16):
    entries = jax.random.normal(stream_key, shape, jnp.float32) * spread
    if len(shards) > 0:
        entries = level_of(stream_key, shape, shards, -0.22, 0.18) * entries
    return jnp.clip(entries, min=-reach, max=reach).astype(kind)


def setup_inputs(seed: int = 0) -> dict:
    splits = jax.random.split(jax.random.key(seed), 11)
    return {
        "tokens": centred(splits[0], (SEQS, LENGTH, D), 1.0, 6.0, ((0, 4), (1, 4))),
        "qkv_weight": centred(splits[1], (D, 3, D), D ** -0.5, 0.21875, ((0, 16), (2, 2))),
        "qv_bias": centred(splits[2], (2, D), 0.5, 3.0, ((1, 2),)),
        "out_weight": centred(splits[3], (D, D), ((LENGTH // 3) ** 0.5 * D ** -0.5), 8.0, ((0, 16), (1, 2))),
        "up_weight": centred(splits[4], (D, FF), D ** -0.5, 0.21875, ((0, 16), (1, 2))),
        "up_bias": centred(splits[5], (FF,), 0.5, 3.0, ((0, 2),)),
        "down_weight": centred(splits[6], (D, FF), FF ** -0.5, 0.109375, ((0, 16), (1, 2))),
        "norm_gains": jnp.clip(1.0 + 0.1 * jax.random.normal(splits[7], (D, 2), jnp.float32), 0.5, 1.5).astype(jnp.bfloat16),
        "row_biases": centred(splits[8], (D, 4), 0.5, 3.0, ((0, 16),)),
        "cotangent": centred(splits[9], (SEQS, LENGTH, D), 1.0, 6.0, ((0, 4), (1, 4))),
    }


@jax.custom_vjp
def low(v):
    return lax.optimization_barrier(v.astype(jnp.bfloat16)).astype(jnp.float32)

@jax.custom_vjp
def low_back(v):
    return v

def low_keep(v):
    return (low(v), None)

def low_pass(kept, grad):
    return (grad,)

def back_keep(v):
    return (v, None)

def back_low(kept, grad):
    return (low(grad),)
low.defvjp(low_keep, low_pass)
low_back.defvjp(back_keep, back_low)
highest = lax.Precision.HIGHEST
epsilon = 1e-12
score_scale = 0.125

def matmul(left, right):
    return jnp.dot(left, right, precision=highest)

def layer_norm(hidden, gain, shift):
    center = hidden - lax.optimization_barrier(jnp.mean(hidden, axis=-1, keepdims=True))
    inv_scale = lax.rsqrt(lax.optimization_barrier(jnp.mean(center * center, axis=-1, keepdims=True)) + epsilon)
    return center * inv_scale * gain + shift

def attend(queries, keys_all, values_all):

    def one_block(query_block):
        scores = low_back(jnp.einsum('qhd,khd->hqk', query_block, keys_all, precision=highest) * score_scale)
        row_max = lax.optimization_barrier(jnp.max(scores, axis=-1, keepdims=True))
        expo = jnp.exp(scores - row_max)
        weights = low(expo / lax.optimization_barrier(jnp.sum(expo, axis=-1, keepdims=True)))
        return jnp.einsum('hqk,khd->qhd', weights, values_all, precision=highest)
    rows = queries.shape[0]
    block_len = min(512, rows)
    blocks = queries.reshape(rows // block_len, block_len, queries.shape[1], queries.shape[2])
    return lax.map(jax.checkpoint(one_block), blocks).reshape(queries.shape)

def forward(seq_tokens, qkv_weight, qv_bias, out_weight, up_weight, up_bias, down_weight, norm_gains, row_biases):
    length = seq_tokens.shape[0]
    queries = low(low_back(matmul(seq_tokens, qkv_weight[:, 0, :]) + qv_bias[0]))
    keys_all = low(low_back(matmul(seq_tokens, qkv_weight[:, 1, :])))
    values_all = low(low_back(matmul(seq_tokens, qkv_weight[:, 2, :]) + qv_bias[1]))
    mixed = attend(queries.reshape(length, H, HD), keys_all.reshape(length, H, HD), values_all.reshape(length, H, HD))
    mixed = low(low_back(mixed.reshape(length, D)))
    attn_out = low_back(matmul(mixed, out_weight.T) + row_biases[:, 0])
    first_out = layer_norm(seq_tokens + attn_out, norm_gains[:, 0], row_biases[:, 1])
    inner_pre = low_back(matmul(low(first_out), up_weight) + up_bias)
    activated = low(jax.nn.gelu(inner_pre, approximate=False))
    ffn_out = low_back(matmul(activated, down_weight.T) + row_biases[:, 2])
    return layer_norm(first_out + ffn_out, norm_gains[:, 1], row_biases[:, 3])

def reference(tokens, qkv_weight, qv_bias, out_weight, up_weight, up_bias, down_weight, norm_gains, row_biases, cotangent):
    params = tuple((weight_arr.astype(jnp.float32) for weight_arr in (qkv_weight, qv_bias, out_weight, up_weight, up_bias, down_weight, norm_gains, row_biases)))

    def one_sequence(totals, seq_pair):
        seq_tokens, seq_cot = seq_pair
        layer_out, pullback = jax.vjp(forward, seq_tokens.astype(jnp.float32), *params)
        gradients = pullback(seq_cot.astype(jnp.float32))
        totals = tuple((left_sum + right_term for left_sum, right_term in zip(totals, gradients[1:])))
        return (totals, (layer_out.astype(jnp.bfloat16), gradients[0].astype(jnp.bfloat16)))
    zero_grads = tuple((jnp.zeros_like(weight_arr) for weight_arr in params))
    totals, (outputs, token_grads) = lax.scan(one_sequence, zero_grads, (tokens, cotangent))
    return (outputs, token_grads, totals[0], totals[1], totals[2], totals[3], totals[4], totals[5], totals[6], totals[7])
```

```python
import jax
import jax.numpy as jnp
from jax import lax
from jax.experimental import pallas as pl
from jax.experimental.pallas import tpu as pltpu
from jax.sharding import PartitionSpec as P

HD = 64
B = jnp.bfloat16
F = jnp.float32
epsilon = 1e-12
score_scale = 0.125
LOG2E = 1.4426950408889634
WEIGHT_AXES = ("tp", "fsdp", "ctx")


def dot(left, right, left_dim, right_dim):
    return lax.dot_general(
        left, right, (((left_dim,), (right_dim,)), ((), ())), preferred_element_type=F
    )


def split_low(value, count):
    parts = []
    for _ in range(count):
        part = value.astype(B)
        parts.append(part)
        value = value - part.astype(F)
    return parts


def pick_block(size, wanted):
    while size % wanted:
        wanted //= 2
    return wanted


def forward_kernel(q_ref, kv_ref, o_ref, lse_ref, qx, kx, vx, *, bk):
    rows = q_ref.shape[-1]
    keys = kv_ref.shape[-1]
    scaled = q_ref[0].astype(F) * (score_scale * LOG2E)
    high, rest = split_low(scaled, 2)
    qx[0:HD, :] = high
    qx[HD : 2 * HD, :] = rest
    kx[0:HD, :] = kv_ref[0, 0]
    kx[HD : 2 * HD, :] = kv_ref[0, 0]
    vx[0:HD, :] = kv_ref[0, 1]
    vx[HD : HD + 16, :] = jnp.ones((16, keys), B)

    def step(i, carry):
        row_max, mixed = carry
        off = pl.multiple_of(i * bk, bk)
        scores = dot(kx[:, pl.ds(off, bk)], qx[...], 0, 0)
        new_max = jnp.maximum(row_max, jnp.max(scores, axis=0, keepdims=True))
        probs = jnp.exp2(scores - new_max).astype(B)
        mixed = mixed * jnp.exp2(row_max - new_max) + dot(vx[:, pl.ds(off, bk)], probs, 1, 0)
        return new_max, mixed

    start = (jnp.full((1, rows), -jnp.inf, F), jnp.zeros((HD + 16, rows), F))
    row_max, mixed = lax.fori_loop(0, keys // bk, step, start)
    total = mixed[HD : HD + 1, :]
    o_ref[0] = mixed[0:HD, :] / total
    lse_ref[0, 0] = row_max + jnp.log2(total)


def attention_forward(q_t, kv_t, bk):
    parts, width, rows = q_t.shape
    keys = kv_t.shape[3]
    heads = width // HD
    bk = pick_block(keys, bk)
    return pl.pallas_call(
        lambda *refs: forward_kernel(*refs, bk=bk),
        grid=(parts, heads),
        in_specs=[
            pl.BlockSpec((1, HD, rows), lambda t, h: (t, h, 0)),
            pl.BlockSpec((1, 2, HD, keys), lambda t, h: (t, 0, h, 0)),
        ],
        out_specs=[
            pl.BlockSpec((1, HD, rows), lambda t, h: (t, h, 0)),
            pl.BlockSpec((1, 1, 1, rows), lambda t, h: (t, h, 0, 0)),
        ],
        out_shape=[
            jax.ShapeDtypeStruct((parts, width, rows), F),
            jax.ShapeDtypeStruct((parts, heads, 1, rows), F),
        ],
        scratch_shapes=[
            pltpu.VMEM((2 * HD, rows), B),
            pltpu.VMEM((2 * HD, keys), B),
            pltpu.VMEM((HD + 16, keys), B),
        ],
        compiler_params=pltpu.CompilerParams(
            vmem_limit_bytes=56 << 20, dimension_semantics=("arbitrary", "arbitrary")
        ),
        name="attn_forward",
    )(q_t, kv_t)


def backward_kernel(
    q_ref, kv_ref, do_ref, lse_ref, delta_ref, dq_ref, dkv_ref, qx, kx, dx, vx, dq_acc, *, bk, bq
):
    rows = q_ref.shape[-1]
    keys = kv_ref.shape[-1]
    scaled = q_ref[0].astype(F) * (score_scale * LOG2E)
    high, rest = split_low(scaled, 2)
    sub = lax.broadcasted_iota(jnp.int32, (16, rows), 0)

    def stacked(value):
        block = jnp.zeros((16, rows), F)
        for j, part in enumerate(split_low(value, 3)):
            block = jnp.where(sub == j, jnp.broadcast_to(part.astype(F), (16, rows)), block)
        return block.astype(B)

    qx[0:HD, :] = high
    qx[HD : 2 * HD, :] = rest
    qx[2 * HD : 2 * HD + 16, :] = stacked(lse_ref[0, 0])
    dx[0:HD, :] = do_ref[0]
    dx[HD : HD + 16, :] = stacked(delta_ref[0, 0])
    kx[0:HD, :] = kv_ref[0, 0]
    kx[HD : 2 * HD, :] = kv_ref[0, 0]
    kx[2 * HD : 2 * HD + 16, :] = jnp.full((16, keys), -1.0, B)
    vx[0:HD, :] = kv_ref[0, 1]
    vx[HD : HD + 16, :] = jnp.full((16, keys), -1.0, B)
    dq_acc[...] = jnp.zeros_like(dq_acc)

    def step(i, carry):
        off = pl.multiple_of(i * bk, bk)
        k_part = kx[:, pl.ds(off, bk)]
        v_part = vx[:, pl.ds(off, bk)]
        dk_part = jnp.zeros((HD, bk), F)
        dv_part = jnp.zeros((HD, bk), F)
        for j in range(0, rows, bq):
            probs = jnp.exp2(dot(qx[:, j : j + bq], k_part, 0, 0))
            prob_grad = dot(dx[:, j : j + bq], v_part, 0, 0)
            score_low = (probs * prob_grad).astype(B)
            prob_low = probs.astype(B)
            dv_part = dv_part + dot(dx[0:HD, j : j + bq], prob_low, 1, 0)
            dk_part = dk_part + dot(q_ref[0, :, j : j + bq], score_low, 1, 0)
            dq_acc[j : j + bq, :] += dot(score_low, k_part[0:HD, :], 1, 1)
        dkv_ref[0, 0, :, pl.ds(off, bk)] = (dk_part * score_scale).astype(B)
        dkv_ref[0, 1, :, pl.ds(off, bk)] = dv_part.astype(B)
        return carry

    lax.fori_loop(0, keys // bk, step, 0)
    dq_ref[0] = jnp.transpose(dq_acc[...] * score_scale).astype(dq_ref.dtype)


def attention_backward(q_t, kv_t, do_t, lse, delta, bk, bq, dq_type):
    parts, width, rows = q_t.shape
    keys = kv_t.shape[3]
    heads = width // HD
    bk = pick_block(keys, bk)
    bq = pick_block(rows, bq)
    row_spec = pl.BlockSpec((1, HD, rows), lambda t, h: (t, h, 0))
    stat_spec = pl.BlockSpec((1, 1, 1, rows), lambda t, h: (t, h, 0, 0))
    key_spec = pl.BlockSpec((1, 2, HD, keys), lambda t, h: (t, 0, h, 0))
    return pl.pallas_call(
        lambda *refs: backward_kernel(*refs, bk=bk, bq=bq),
        grid=(parts, heads),
        in_specs=[row_spec, key_spec, row_spec, stat_spec, stat_spec],
        out_specs=[row_spec, key_spec],
        out_shape=[
            jax.ShapeDtypeStruct((parts, width, rows), dq_type),
            jax.ShapeDtypeStruct((parts, 2, width, keys), B),
        ],
        scratch_shapes=[
            pltpu.VMEM((2 * HD + 16, rows), B),
            pltpu.VMEM((2 * HD + 16, keys), B),
            pltpu.VMEM((HD + 16, rows), B),
            pltpu.VMEM((HD + 16, keys), B),
            pltpu.VMEM((rows, HD), F),
        ],
        compiler_params=pltpu.CompilerParams(
            vmem_limit_bytes=56 << 20, dimension_semantics=("arbitrary", "arbitrary")
        ),
        name="attn_backward",
    )(q_t, kv_t, do_t, lse, delta)


def ring_gather(block):
    count = lax.axis_size("ctx")
    up = [(i, (i + 1) % count) for i in range(count)]
    down = [((i + 1) % count, i) for i in range(count)]
    half = block.shape[0] // 2
    first, second = block[:half], block[half:]
    pieces = []
    for _ in range(count - 1):
        first = lax.ppermute(first, "ctx", up)
        second = lax.ppermute(second, "ctx", down)
        pieces.append((first, second))
    return pieces


def ring_reduce(pieces):
    count = lax.axis_size("ctx")
    up = [(i, (i + 1) % count) for i in range(count)]
    down = [((i + 1) % count, i) for i in range(count)]
    first = second = None
    for one, two in reversed(pieces):
        if first is not None:
            one = one + first.astype(F)
            two = two + second.astype(F)
        first = lax.ppermute(one.astype(B), "ctx", down)
        second = lax.ppermute(two.astype(B), "ctx", up)
    return jnp.concatenate([first, second], axis=0).astype(F)


def sum_all(vector):
    for axis in ("fsdp", "tp", "ctx"):
        size = lax.axis_size(axis)
        bit = 1
        while bit < size:
            vector = vector + lax.ppermute(vector, axis, [(i, i ^ bit) for i in range(size)])
            bit *= 2
    return vector


def tp_gather(vector):
    size = lax.axis_size("tp")
    own = lax.axis_index("tp")
    out = jnp.zeros((size,) + vector.shape, vector.dtype)
    out = lax.dynamic_update_index_in_dim(out, vector, own, 0)
    for shift in range(1, size):
        got = lax.ppermute(vector, "tp", [(i, (i + shift) % size) for i in range(size)])
        out = lax.dynamic_update_index_in_dim(out, got, (own - shift) % size, 0)
    return out


def tp_exchange(rows):
    size = lax.axis_size("tp")
    own = lax.axis_index("tp")
    seqs, length, width = rows.shape
    split = rows.reshape(seqs, size, length // size, width)
    out = jnp.zeros((size, seqs, length // size, width), rows.dtype)
    kept = lax.dynamic_index_in_dim(split, own, 1, keepdims=False)
    out = lax.dynamic_update_index_in_dim(out, kept, own, 0)
    for shift in range(1, size):
        sent = lax.dynamic_index_in_dim(split, (own + shift) % size, 1, keepdims=False)
        got = lax.ppermute(sent, "tp", [(i, (i + shift) % size) for i in range(size)])
        out = lax.dynamic_update_index_in_dim(out, got, (own - shift) % size, 0)
    return out.reshape(size * seqs, length // size, width)


def norm_forward(hidden, gain, shift):
    center = hidden - jnp.mean(hidden, axis=-1, keepdims=True)
    inv_scale = lax.rsqrt(jnp.mean(center * center, axis=-1, keepdims=True) + epsilon)
    normed = center * inv_scale
    return (normed * gain + shift, normed, inv_scale)


def norm_backward(grad_out, normed, inv_scale, gain):
    grad_norm = grad_out * gain
    return inv_scale * (
        grad_norm
        - jnp.mean(grad_norm, axis=-1, keepdims=True)
        - normed * jnp.mean(grad_norm * normed, axis=-1, keepdims=True)
    )


def gelu_exact(values):
    return jax.nn.gelu(values, approximate=False)


def body(
    tokens,
    qkv_weight,
    qv_bias,
    out_weight,
    up_weight,
    up_bias,
    down_weight,
    norm_gains,
    row_biases,
    cotangent,
):
    seq_count, local_len, width = tokens.shape
    tp_count = lax.axis_size("tp")
    own_seqs = seq_count // tp_count
    first_seq = lax.axis_index("tp") * own_seqs
    own_tokens = lax.dynamic_slice_in_dim(tokens, first_seq, own_seqs, 0)
    own_cotangent = lax.dynamic_slice_in_dim(cotangent, first_seq, own_seqs, 0)
    rows = own_seqs * local_len
    x_own = own_tokens.reshape(rows, width)
    shard_rows = qkv_weight.shape[0]
    head_width = qkv_weight.shape[2]
    ff_width = up_weight.shape[1]
    pad = 128 - norm_gains.shape[1] - row_biases.shape[1]

    first_shard = jnp.concatenate(
        [
            qkv_weight.reshape(shard_rows, 3 * head_width),
            norm_gains,
            row_biases,
            jnp.zeros((shard_rows, pad), B),
        ],
        axis=1,
    )
    first_all = lax.all_gather(first_shard, WEIGHT_AXES, axis=0, tiled=True)
    first_all = first_all.reshape(tp_count, width, first_shard.shape[1])
    x_pieces = [ring_gather(own_tokens[s]) for s in range(own_seqs)]
    second_shard = jnp.concatenate([out_weight, up_weight, down_weight], axis=1)
    second_all = lax.all_gather(second_shard, WEIGHT_AXES, axis=0, tiled=True)
    second_all = second_all.reshape(tp_count, width, second_shard.shape[1])
    w_q = first_all[:, :, :head_width]
    w_kv = first_all[:, :, head_width : 3 * head_width]
    rows_all = jnp.transpose(first_all[0, :, 3 * head_width :]).astype(F)
    gain1, gain2 = rows_all[0], rows_all[1]
    out_bias, shift1, down_bias, shift2 = (rows_all[2 + i] for i in range(4))
    w_out = second_all[:, :, :head_width]
    w_up = second_all[:, :, head_width : head_width + ff_width]
    w_down = second_all[:, :, head_width + ff_width :]
    bias_all = tp_gather(jnp.concatenate([qv_bias.reshape(-1), up_bias]))
    q_bias = bias_all[:, :head_width].astype(F)
    v_bias = bias_all[:, head_width : 2 * head_width].astype(F)
    u_bias = bias_all[:, 2 * head_width :].astype(F)
    kv_bias = jnp.concatenate([jnp.zeros_like(v_bias), v_bias], axis=1)

    x_full = [
        jnp.concatenate([own_tokens[s]] + [p for pair in x_pieces[s] for p in pair], axis=0)
        for s in range(own_seqs)
    ]
    q_t = [
        (dot(w_q, own_tokens[s], 1, 1) + q_bias[:, :, None]).astype(B) for s in range(own_seqs)
    ]
    kv_t = [
        (dot(w_kv, x_full[s], 1, 1) + kv_bias[:, :, None])
        .astype(B)
        .reshape(tp_count, 2, head_width, x_full[s].shape[0])
        for s in range(own_seqs)
    ]
    attended = [attention_forward(q_t[s], kv_t[s], 2048) for s in range(own_seqs)]
    om_t = [one[0] for one in attended]
    lse = [one[1] for one in attended]
    mixed_t = jnp.concatenate([one.astype(B) for one in om_t], axis=2)
    attn_part = sum(dot(mixed_t[t], w_out[t], 0, 1) for t in range(tp_count))
    x_float = x_own.astype(F)
    first_out, first_norm, first_scale = norm_forward(
        x_float + attn_part + out_bias, gain1, shift1
    )
    first_low = first_out.astype(B)

    act_low, gelu_back = [], []
    for t in range(tp_count):
        inner = dot(first_low, w_up[t], 1, 0) + u_bias[t]
        activated, back = jax.vjp(gelu_exact, inner)
        act_low.append(activated.astype(B))
        gelu_back.append(back)
    ffn_out = sum(dot(act_low[t], w_down[t], 1, 1) for t in range(tp_count)) + down_bias
    grad_final = own_cotangent.reshape(rows, width).astype(F)
    final_out, final_norm, final_scale = norm_forward(first_out + ffn_out, gain2, shift2)
    output = tp_exchange(final_out.astype(B).reshape(own_seqs, local_len, width))
    gain2_grad = jnp.sum(grad_final * final_norm, axis=0)
    shift2_grad = jnp.sum(grad_final, axis=0)
    grad_second = norm_backward(grad_final, final_norm, final_scale, gain2)
    df = grad_second.astype(B)
    down_bias_grad = jnp.sum(df.astype(F), axis=0)
    inner_low = [
        gelu_back[t](dot(df, w_down[t], 1, 0))[0].astype(B) for t in range(tp_count)
    ]
    up_bias_grad = [jnp.sum(inner_low[t].astype(F), axis=0) for t in range(tp_count)]
    first_grad = grad_second + sum(dot(inner_low[t], w_up[t], 1, 1) for t in range(tp_count))
    gain1_grad = jnp.sum(first_grad * first_norm, axis=0)
    shift1_grad = jnp.sum(first_grad, axis=0)
    resid_grad = norm_backward(first_grad, first_norm, first_scale, gain1)
    da = resid_grad.astype(B)
    out_bias_grad = jnp.sum(da.astype(F), axis=0)
    second_grad = jnp.stack(
        [
            jnp.concatenate(
                [
                    dot(da, mixed_t[t], 0, 1).astype(B),
                    dot(first_low, inner_low[t], 0, 0).astype(B),
                    dot(df, act_low[t], 0, 0).astype(B),
                ],
                axis=1,
            )
            for t in range(tp_count)
        ]
    )
    second_grad = lax.psum_scatter(
        second_grad.reshape(tp_count * width, second_shard.shape[1]),
        WEIGHT_AXES,
        scatter_dimension=0,
        tiled=True,
    ).astype(F)

    do_t = dot(w_out, da, 1, 1).astype(B)
    v_bias_grad = jnp.sum(do_t.astype(F), axis=2)
    early = sum_all(
        jnp.concatenate(
            [gain1_grad, gain2_grad, out_bias_grad, shift1_grad, down_bias_grad, shift2_grad]
            + up_bias_grad
            + [v_bias_grad.reshape(-1)]
        )
    )
    dq_t, dkv_t = [], []
    for s in range(own_seqs):
        do_s = do_t[:, :, s * local_len : (s + 1) * local_len]
        delta = (om_t[s] * do_s.astype(F)).reshape(tp_count, head_width // HD, HD, local_len)
        delta = jnp.sum(delta, axis=2, keepdims=True)
        one_dq, one_dkv = attention_backward(q_t[s], kv_t[s], do_s, lse[s], delta, 1024, 512, B)
        dq_t.append(one_dq)
        dkv_t.append(one_dkv.reshape(tp_count, 2 * head_width, one_dkv.shape[3]))
    q_bias_grad = sum_all(sum(jnp.sum(one.astype(F), axis=2) for one in dq_t).reshape(-1))

    own_grads = []
    half = local_len // 2
    for s in range(own_seqs):
        full = sum(dot(dkv_t[s][t], w_kv[t], 0, 1) for t in range(tp_count))
        pieces = []
        for i in range(len(x_pieces[s])):
            at = local_len + i * local_len
            pieces.append((full[at : at + half], full[at + half : at + local_len]))
        own = full[:local_len] + sum(dot(dq_t[s][t], w_q[t], 0, 1) for t in range(tp_count))
        own_grads.append(own + ring_reduce(pieces))
    tokens_grad = resid_grad.reshape(own_seqs, local_len, width) + jnp.stack(own_grads)
    tokens_out = tp_exchange(tokens_grad.astype(B))
    qkv_grad = jnp.stack(
        [
            jnp.concatenate(
                [
                    sum(dot(own_tokens[s], dq_t[s][t], 0, 1) for s in range(own_seqs)).astype(B),
                    sum(dot(x_full[s], dkv_t[s][t], 0, 1) for s in range(own_seqs)).astype(B),
                ],
                axis=1,
            )
            for t in range(tp_count)
        ]
    )
    qkv_grad = lax.psum_scatter(
        qkv_grad.reshape(tp_count * width, 3 * head_width),
        WEIGHT_AXES,
        scatter_dimension=0,
        tiled=True,
    ).astype(F)

    member = lax.axis_index("fsdp") * lax.axis_size("ctx") + lax.axis_index("ctx")
    own_tp = lax.axis_index("tp")
    six = lax.dynamic_slice_in_dim(
        early[: 6 * width].reshape(6, width), member * shard_rows, shard_rows, 1
    )
    six = jnp.transpose(six)
    up_total = lax.dynamic_slice_in_dim(early, 6 * width + own_tp * ff_width, ff_width, 0)
    v_total = lax.dynamic_slice_in_dim(
        early, 6 * width + tp_count * ff_width + own_tp * head_width, head_width, 0
    )
    q_total = lax.dynamic_slice_in_dim(q_bias_grad, own_tp * head_width, head_width, 0)
    return (
        output,
        tokens_out,
        qkv_grad.reshape(shard_rows, 3, head_width),
        jnp.stack([q_total, v_total]),
        second_grad[:, :head_width],
        second_grad[:, head_width : head_width + ff_width],
        up_total,
        second_grad[:, head_width + ff_width :],
        six[:, :2],
        six[:, 2:],
    )


def solution(mesh):
    in_specs = (
        P("fsdp", "ctx", None),
        P(("fsdp", "ctx"), None, "tp"),
        P(None, "tp"),
        P(("fsdp", "ctx"), "tp"),
        P(("fsdp", "ctx"), "tp"),
        P("tp"),
        P(("fsdp", "ctx"), "tp"),
        P(("fsdp", "ctx"), None),
        P(("fsdp", "ctx"), None),
        P("fsdp", "ctx", None),
    )
    out_specs = (
        P("fsdp", ("ctx", "tp"), None),
        P("fsdp", ("ctx", "tp"), None),
        P(("fsdp", "ctx"), None, "tp"),
        P(None, "tp"),
        P(("fsdp", "ctx"), "tp"),
        P(("fsdp", "ctx"), "tp"),
        P("tp"),
        P(("fsdp", "ctx"), "tp"),
        P(("fsdp", "ctx"), None),
        P(("fsdp", "ctx"), None),
    )
    return jax.shard_map(body, mesh=mesh, in_specs=in_specs, out_specs=out_specs, check_vma=False)
```

```python
import jax
import jax.numpy as jnp
from jax import lax
from jax.experimental import pallas as pl
from jax.experimental.pallas import tpu as pltpu
from jax.sharding import PartitionSpec as P

HD = 64
B = jnp.bfloat16
F = jnp.float32
epsilon = 1e-12
score_scale = 0.125
LOG2E = 1.4426950408889634
WEIGHT_AXES = ("tp", "fsdp", "ctx")


def dot(left, right, left_dim, right_dim):
    return lax.dot_general(
        left, right, (((left_dim,), (right_dim,)), ((), ())), preferred_element_type=F
    )


def split_low(value, count):
    parts = []
    for _ in range(count):
        part = value.astype(B)
        parts.append(part)
        value = value - part.astype(F)
    return parts


def pick_block(size, wanted):
    while size % wanted:
        wanted //= 2
    return wanted


def forward_kernel(*refs, chunks, first, last, bk):
    q_ref = refs[0]
    kv_refs = refs[1 : 1 + chunks]
    at = 1 + chunks
    if not first:
        o_in, stat_in = refs[at : at + 2]
        at += 2
    o_ref, stat_ref, qx, kx, vx = refs[at:]
    rows = q_ref.shape[-1]
    keys = kx.shape[-1]
    scaled = q_ref[0].astype(F) * (score_scale * LOG2E)
    high, rest = split_low(scaled, 2)
    qx[0:HD, :] = high
    qx[HD : 2 * HD, :] = rest
    size = keys // chunks
    for c, kv_ref in enumerate(kv_refs):
        at = c * size
        kx[0:HD, at : at + size] = kv_ref[0, 0]
        kx[HD : 2 * HD, at : at + size] = kv_ref[0, 0]
        vx[0:HD, at : at + size] = kv_ref[0, 1]
    vx[HD : HD + 16, :] = jnp.ones((16, keys), B)

    def step(i, carry):
        row_max, mixed, total = carry
        off = pl.multiple_of(i * bk, bk)
        scores = dot(kx[:, pl.ds(off, bk)], qx[...], 0, 0)
        new_max = jnp.maximum(row_max, jnp.max(scores, axis=0, keepdims=True))
        probs = jnp.exp2(scores - new_max).astype(B)
        scale = jnp.exp2(row_max - new_max)
        more = dot(vx[:, pl.ds(off, bk)], probs, 1, 0)
        return new_max, mixed * scale + more[0:HD, :], total * scale + more[HD : HD + 1, :]

    if first:
        start = (
            jnp.full((1, rows), -jnp.inf, F),
            jnp.zeros((HD, rows), F),
            jnp.zeros((1, rows), F),
        )
    else:
        start = (stat_in[0, 0, 0:1, :], o_in[0], stat_in[0, 0, 1:2, :])
    row_max, mixed, total = lax.fori_loop(0, keys // bk, step, start)
    if last:
        o_ref[0] = mixed / total
        stat_ref[0, 0] = row_max + jnp.log2(total)
    else:
        o_ref[0] = mixed
        stat_ref[0, 0, 0:1, :] = row_max
        stat_ref[0, 0, 1:2, :] = total


def attention_forward(q_t, kv_list, state, last, bk):
    parts, width, rows = q_t.shape
    chunks = len(kv_list)
    keys = kv_list[0].shape[3]
    heads = width // HD
    bk = pick_block(keys * chunks, bk)
    first = state is None
    row_spec = pl.BlockSpec((1, HD, rows), lambda t, h: (t, h, 0))
    two_spec = pl.BlockSpec((1, 1, 2, rows), lambda t, h: (t, h, 0, 0))
    one_spec = pl.BlockSpec((1, 1, 1, rows), lambda t, h: (t, h, 0, 0))
    key_spec = pl.BlockSpec((1, 2, HD, keys), lambda t, h: (t, 0, h, 0))
    total = parts * heads * rows * keys * chunks
    return pl.pallas_call(
        lambda *refs: forward_kernel(*refs, chunks=chunks, first=first, last=last, bk=bk),
        grid=(parts, heads),
        in_specs=[row_spec] + [key_spec] * chunks + ([] if first else [row_spec, two_spec]),
        out_specs=[row_spec, one_spec if last else two_spec],
        out_shape=[
            jax.ShapeDtypeStruct((parts, width, rows), F),
            jax.ShapeDtypeStruct((parts, heads, 1 if last else 2, rows), F),
        ],
        scratch_shapes=[
            pltpu.VMEM((2 * HD, rows), B),
            pltpu.VMEM((2 * HD, keys * chunks), B),
            pltpu.VMEM((HD + 16, keys * chunks), B),
        ],
        compiler_params=pltpu.CompilerParams(
            vmem_limit_bytes=56 << 20, dimension_semantics=("arbitrary", "arbitrary")
        ),
        cost_estimate=pl.CostEstimate(
            flops=1024 * total, transcendentals=total, bytes_accessed=16 << 20
        ),
        name="attn_forward",
    )(q_t, *kv_list, *(() if first else state))


def backward_kernel(
    q_ref,
    kv_ref,
    do_ref,
    lse_ref,
    delta_ref,
    dq_in,
    dq_ref,
    dkv_ref,
    qx,
    kx,
    dx,
    vx,
    dq_acc,
    *,
    bk,
    bq,
):
    rows = q_ref.shape[-1]
    keys = kv_ref.shape[-1]
    scaled = q_ref[0].astype(F) * (score_scale * LOG2E)
    high, rest = split_low(scaled, 2)
    sub = lax.broadcasted_iota(jnp.int32, (16, rows), 0)

    def stacked(value):
        block = jnp.zeros((16, rows), F)
        for j, part in enumerate(split_low(value, 3)):
            block = jnp.where(sub == j, jnp.broadcast_to(part.astype(F), (16, rows)), block)
        return block.astype(B)

    qx[0:HD, :] = high
    qx[HD : 2 * HD, :] = rest
    qx[2 * HD : 2 * HD + 16, :] = stacked(lse_ref[0, 0])
    dx[0:HD, :] = do_ref[0]
    dx[HD : HD + 16, :] = stacked(delta_ref[0, 0])
    kx[0:HD, :] = kv_ref[0, 0]
    kx[HD : 2 * HD, :] = kv_ref[0, 0]
    kx[2 * HD : 2 * HD + 16, :] = jnp.full((16, keys), -1.0, B)
    vx[0:HD, :] = kv_ref[0, 1]
    vx[HD : HD + 16, :] = jnp.full((16, keys), -1.0, B)
    dq_acc[...] = jnp.zeros_like(dq_acc)

    def step(i, carry):
        off = pl.multiple_of(i * bk, bk)
        k_part = kx[:, pl.ds(off, bk)]
        v_part = vx[:, pl.ds(off, bk)]
        dk_part = jnp.zeros((HD, bk), F)
        dv_part = jnp.zeros((HD, bk), F)
        for j in range(0, rows, bq):
            probs = jnp.exp2(dot(qx[:, j : j + bq], k_part, 0, 0))
            prob_grad = dot(dx[:, j : j + bq], v_part, 0, 0)
            score_low = (probs * prob_grad).astype(B)
            prob_low = probs.astype(B)
            dv_part = dv_part + dot(dx[0:HD, j : j + bq], prob_low, 1, 0)
            dk_part = dk_part + dot(q_ref[0, :, j : j + bq], score_low, 1, 0)
            dq_acc[j : j + bq, :] += dot(score_low, k_part[0:HD, :], 1, 1)
        dkv_ref[0, 0, :, pl.ds(off, bk)] = (dk_part * score_scale).astype(B)
        dkv_ref[0, 1, :, pl.ds(off, bk)] = dv_part.astype(B)
        return carry

    lax.fori_loop(0, keys // bk, step, 0)
    dq_ref[0] = dq_in[0] + jnp.transpose(dq_acc[...] * score_scale)


def attention_backward(q_t, kv_t, do_t, lse, delta, dq_t, bk, bq):
    parts, width, rows = q_t.shape
    keys = kv_t.shape[3]
    heads = width // HD
    bk = pick_block(keys, bk)
    bq = pick_block(rows, bq)
    total = parts * heads * rows * keys
    row_spec = pl.BlockSpec((1, HD, rows), lambda t, h: (t, h, 0))
    stat_spec = pl.BlockSpec((1, 1, 1, rows), lambda t, h: (t, h, 0, 0))
    key_spec = pl.BlockSpec((1, 2, HD, keys), lambda t, h: (t, 0, h, 0))
    return pl.pallas_call(
        lambda *refs: backward_kernel(*refs, bk=bk, bq=bq),
        grid=(parts, heads),
        in_specs=[row_spec, key_spec, row_spec, stat_spec, stat_spec, row_spec],
        out_specs=[row_spec, key_spec],
        out_shape=[
            jax.ShapeDtypeStruct((parts, width, rows), F),
            jax.ShapeDtypeStruct((parts, 2, width, keys), B),
        ],
        scratch_shapes=[
            pltpu.VMEM((2 * HD + 16, rows), B),
            pltpu.VMEM((2 * HD + 16, keys), B),
            pltpu.VMEM((HD + 16, rows), B),
            pltpu.VMEM((HD + 16, keys), B),
            pltpu.VMEM((rows, HD), F),
        ],
        compiler_params=pltpu.CompilerParams(
            vmem_limit_bytes=56 << 20, dimension_semantics=("arbitrary", "arbitrary")
        ),
        cost_estimate=pl.CostEstimate(
            flops=2048 * total, transcendentals=total, bytes_accessed=16 << 20
        ),
        input_output_aliases={5: 0},
        name="attn_backward",
    )(q_t, kv_t, do_t, lse, delta, dq_t)


def ring_gather(block):
    count = lax.axis_size("ctx")
    up = [(i, (i + 1) % count) for i in range(count)]
    down = [((i + 1) % count, i) for i in range(count)]
    half = block.shape[0] // 2
    first, second = block[:half], block[half:]
    pieces = []
    for _ in range(count - 1):
        first = lax.ppermute(first, "ctx", up)
        second = lax.ppermute(second, "ctx", down)
        pieces.append((first, second))
    return pieces


def ring_return(first, second):
    count = lax.axis_size("ctx")
    up = [(i, (i + 1) % count) for i in range(count)]
    down = [((i + 1) % count, i) for i in range(count)]
    return lax.ppermute(first, "ctx", down), lax.ppermute(second, "ctx", up)


def scatter_sum(blocks, order):
    sizes = {axis: lax.axis_size(axis) for axis in WEIGHT_AXES}
    bits = []
    for axis in WEIGHT_AXES:
        bit = sizes[axis] // 2
        while bit:
            bits.append((axis, bit))
            bit //= 2
    left = blocks.reshape((2,) * len(bits) + blocks.shape[2:])
    todo = sorted(
        bits,
        key=lambda one: (one != ("fsdp", 1), order.index(one[0]), -one[1]),
    )
    for axis, bit in todo:
        dim = bits.index((axis, bit))
        bits.remove((axis, bit))
        mine = (lax.axis_index(axis) // bit) % 2
        sent = lax.dynamic_index_in_dim(left, 1 - mine, dim, keepdims=False)
        kept = lax.dynamic_index_in_dim(left, mine, dim, keepdims=False)
        got = lax.ppermute(sent, axis, [(i, i ^ bit) for i in range(sizes[axis])])
        total = kept.astype(F) + got.astype(F)
        left = total.astype(B) if bits else total
    return left


def sum_all(vector):
    for axis in ("fsdp", "tp", "ctx"):
        size = lax.axis_size(axis)
        bit = 1
        while bit < size:
            vector = vector + lax.ppermute(vector, axis, [(i, i ^ bit) for i in range(size)])
            bit *= 2
    return vector


def tp_gather(vector):
    size = lax.axis_size("tp")
    own = lax.axis_index("tp")
    out = jnp.zeros((size,) + vector.shape, vector.dtype)
    out = lax.dynamic_update_index_in_dim(out, vector, own, 0)
    for shift in range(1, size):
        got = lax.ppermute(vector, "tp", [(i, (i + shift) % size) for i in range(size)])
        out = lax.dynamic_update_index_in_dim(out, got, (own - shift) % size, 0)
    return out


def tp_exchange(rows):
    size = lax.axis_size("tp")
    own = lax.axis_index("tp")
    seqs, length, width = rows.shape
    split = rows.reshape(seqs, size, length // size, width)
    out = jnp.zeros((size, seqs, length // size, width), rows.dtype)
    kept = lax.dynamic_index_in_dim(split, own, 1, keepdims=False)
    out = lax.dynamic_update_index_in_dim(out, kept, own, 0)
    for shift in range(1, size):
        sent = lax.dynamic_index_in_dim(split, (own + shift) % size, 1, keepdims=False)
        got = lax.ppermute(sent, "tp", [(i, (i + shift) % size) for i in range(size)])
        out = lax.dynamic_update_index_in_dim(out, got, (own - shift) % size, 0)
    return out.reshape(size * seqs, length // size, width)


def norm_forward(hidden, gain, shift):
    center = hidden - jnp.mean(hidden, axis=-1, keepdims=True)
    inv_scale = lax.rsqrt(jnp.mean(center * center, axis=-1, keepdims=True) + epsilon)
    normed = center * inv_scale
    return (normed * gain + shift, normed, inv_scale)


def norm_backward(grad_out, normed, inv_scale, gain):
    grad_norm = grad_out * gain
    return inv_scale * (
        grad_norm
        - jnp.mean(grad_norm, axis=-1, keepdims=True)
        - normed * jnp.mean(grad_norm * normed, axis=-1, keepdims=True)
    )


def gelu_exact(values):
    return jax.nn.gelu(values, approximate=False)


def body(
    tokens,
    qkv_weight,
    qv_bias,
    out_weight,
    up_weight,
    up_bias,
    down_weight,
    norm_gains,
    row_biases,
    cotangent,
):
    seq_count, local_len, width = tokens.shape
    tp_count = lax.axis_size("tp")
    own_seqs = seq_count // tp_count
    first_seq = lax.axis_index("tp") * own_seqs
    own_tokens = lax.dynamic_slice_in_dim(tokens, first_seq, own_seqs, 0)
    own_cotangent = lax.dynamic_slice_in_dim(cotangent, first_seq, own_seqs, 0)
    rows = own_seqs * local_len
    x_own = own_tokens.reshape(rows, width)
    shard_rows = qkv_weight.shape[0]
    head_width = qkv_weight.shape[2]
    ff_width = up_weight.shape[1]
    pad = 128 - norm_gains.shape[1] - row_biases.shape[1]

    first_shard = jnp.concatenate(
        [
            qkv_weight.reshape(shard_rows, 3 * head_width),
            norm_gains,
            row_biases,
            jnp.zeros((shard_rows, pad), B),
        ],
        axis=1,
    )
    first_all = lax.all_gather(first_shard, WEIGHT_AXES, axis=0, tiled=True)
    first_all = first_all.reshape(tp_count, width, first_shard.shape[1])
    x_pieces = [ring_gather(own_tokens[s]) for s in range(own_seqs)]
    second_shard = jnp.concatenate([out_weight, up_weight, down_weight], axis=1)
    second_all = lax.all_gather(second_shard, WEIGHT_AXES, axis=0, tiled=True)
    second_all = second_all.reshape(tp_count, width, second_shard.shape[1])
    w_q = first_all[:, :, :head_width]
    w_kv = first_all[:, :, head_width : 3 * head_width]
    rows_all = jnp.transpose(first_all[0, :, 3 * head_width :]).astype(F)
    gain1, gain2 = rows_all[0], rows_all[1]
    out_bias, shift1, down_bias, shift2 = (rows_all[2 + i] for i in range(4))
    w_out = second_all[:, :, :head_width]
    w_up = second_all[:, :, head_width : head_width + ff_width]
    w_down = second_all[:, :, head_width + ff_width :]
    bias_all = tp_gather(jnp.concatenate([qv_bias.reshape(-1), up_bias]))
    q_bias = bias_all[:, :head_width].astype(F)
    v_bias = bias_all[:, head_width : 2 * head_width].astype(F)
    u_bias = bias_all[:, 2 * head_width :].astype(F)
    kv_bias = jnp.concatenate([jnp.zeros_like(v_bias), v_bias], axis=1)

    def project(block):
        got = (dot(w_kv, block, 1, 1) + kv_bias[:, :, None]).astype(B)
        return got.reshape(tp_count, 2, head_width, block.shape[0])

    x_chunks = [
        [own_tokens[s]] + [jnp.concatenate(pair, axis=0) for pair in x_pieces[s]]
        for s in range(own_seqs)
    ]
    chunk_count = len(x_chunks[0])
    near = (chunk_count + 1) // 2
    q_t, kv_t, om_t, lse = [], [], [], []
    for s in range(own_seqs):
        q_s = (dot(w_q, own_tokens[s], 1, 1) + q_bias[:, :, None]).astype(B)
        kv_s = [project(block) for block in x_chunks[s][:near]]
        if near < chunk_count:
            state = attention_forward(q_s, kv_s, None, False, 2048)
            kv_far = [project(block) for block in x_chunks[s][near:]]
            done = attention_forward(q_s, kv_far, state, True, 2048)
            kv_s = kv_s + kv_far
        else:
            done = attention_forward(q_s, kv_s, None, True, 2048)
        q_t.append(q_s)
        kv_t.append(kv_s)
        om_t.append(done[0])
        lse.append(done[1])
    mixed_t = jnp.concatenate([one.astype(B) for one in om_t], axis=2)
    attn_part = sum(dot(mixed_t[t], w_out[t], 0, 1) for t in range(tp_count))
    x_float = x_own.astype(F)
    first_out, first_norm, first_scale = norm_forward(
        x_float + attn_part + out_bias, gain1, shift1
    )
    first_low = first_out.astype(B)

    act_low, gelu_back = [], []
    for t in range(tp_count):
        inner = dot(first_low, w_up[t], 1, 0) + u_bias[t]
        activated, back = jax.vjp(gelu_exact, inner)
        act_low.append(activated.astype(B))
        gelu_back.append(back)
    ffn_out = sum(dot(act_low[t], w_down[t], 1, 1) for t in range(tp_count)) + down_bias
    grad_final = own_cotangent.reshape(rows, width).astype(F)
    final_out, final_norm, final_scale = norm_forward(first_out + ffn_out, gain2, shift2)
    output = tp_exchange(final_out.astype(B).reshape(own_seqs, local_len, width))
    gain2_grad = jnp.sum(grad_final * final_norm, axis=0)
    shift2_grad = jnp.sum(grad_final, axis=0)
    grad_second = norm_backward(grad_final, final_norm, final_scale, gain2)
    df = grad_second.astype(B)
    down_bias_grad = jnp.sum(df.astype(F), axis=0)
    inner_low = [
        gelu_back[t](dot(df, w_down[t], 1, 0))[0].astype(B) for t in range(tp_count)
    ]
    up_bias_grad = [jnp.sum(inner_low[t].astype(F), axis=0) for t in range(tp_count)]
    first_grad = grad_second + sum(dot(inner_low[t], w_up[t], 1, 1) for t in range(tp_count))
    gain1_grad = jnp.sum(first_grad * first_norm, axis=0)
    shift1_grad = jnp.sum(first_grad, axis=0)
    resid_grad = norm_backward(first_grad, first_norm, first_scale, gain1)
    da = resid_grad.astype(B)
    out_bias_grad = jnp.sum(da.astype(F), axis=0)
    second_grad = jnp.stack(
        [
            jnp.concatenate(
                [
                    dot(da, mixed_t[t], 0, 1).astype(B),
                    dot(first_low, inner_low[t], 0, 0).astype(B),
                    dot(df, act_low[t], 0, 0).astype(B),
                ],
                axis=1,
            )
            for t in range(tp_count)
        ]
    )
    do_t = dot(w_out, da, 1, 1).astype(B)
    do_t, second_grad = lax.optimization_barrier((do_t, second_grad))
    second_grad = lax.psum_scatter(
        second_grad.reshape(tp_count * width, second_shard.shape[1]),
        WEIGHT_AXES,
        scatter_dimension=0,
        tiled=True,
    ).astype(F)

    v_bias_grad = jnp.sum(do_t.astype(F), axis=2)
    early = sum_all(
        jnp.concatenate(
            [gain1_grad, gain2_grad, out_bias_grad, shift1_grad, down_bias_grad, shift2_grad]
            + up_bias_grad
            + [v_bias_grad.reshape(-1)]
        )
    )
    kv_grad = [0.0] * tp_count
    q_grad = [0.0] * tp_count
    q_bias_grad = 0.0
    own_grads = []
    half = local_len // 2
    for s in range(own_seqs):
        do_s = do_t[:, :, s * local_len : (s + 1) * local_len]
        delta = (om_t[s] * do_s.astype(F)).reshape(tp_count, head_width // HD, HD, local_len)
        delta = jnp.sum(delta, axis=2, keepdims=True)
        dq = jnp.zeros(om_t[s].shape, F)
        got = None
        for c in reversed(range(chunk_count)):
            dq, dkv = attention_backward(q_t[s], kv_t[s][c], do_s, lse[s], delta, dq, 1024, 512)
            dkv = dkv.reshape(tp_count, 2 * head_width, dkv.shape[3])
            part = sum(dot(dkv[t], w_kv[t], 0, 1) for t in range(tp_count))
            kv_grad = [kv_grad[t] + dot(x_chunks[s][c], dkv[t], 0, 1) for t in range(tp_count)]
            if c:
                one, two = part[:half], part[half:]
                if got is not None:
                    one = one + got[0].astype(F)
                    two = two + got[1].astype(F)
                one, two, dq, *kv_grad = lax.optimization_barrier(
                    (one.astype(B), two.astype(B), dq, *kv_grad)
                )
                got = ring_return(one, two)
        dq_low = dq.astype(B)
        q_bias_grad = q_bias_grad + jnp.sum(dq_low.astype(F), axis=2)
        q_grad = [q_grad[t] + dot(own_tokens[s], dq_low[t], 0, 1) for t in range(tp_count)]
        part = part + sum(dot(dq_low[t], w_q[t], 0, 1) for t in range(tp_count))
        if got is not None:
            part = part + jnp.concatenate(got, axis=0).astype(F)
        own_grads.append(part)
    q_bias_grad = sum_all(q_bias_grad.reshape(-1))
    qkv_grad = jnp.stack(
        [jnp.concatenate([q_grad[t], kv_grad[t]], axis=1).astype(B) for t in range(tp_count)]
    )
    qkv_grad = qkv_grad.reshape(tp_count, width // shard_rows, shard_rows, 3 * head_width)
    cut = (3 * head_width // 256) * 128
    qkv_grad = jnp.concatenate(
        [
            scatter_sum(qkv_grad[..., :cut], ("tp", "fsdp", "ctx")),
            scatter_sum(qkv_grad[..., cut:], ("fsdp", "tp", "ctx")),
        ],
        axis=1,
    )
    tokens_grad = resid_grad.reshape(own_seqs, local_len, width) + jnp.stack(own_grads)
    tokens_out = tp_exchange(tokens_grad.astype(B))

    member = lax.axis_index("fsdp") * lax.axis_size("ctx") + lax.axis_index("ctx")
    own_tp = lax.axis_index("tp")
    six = lax.dynamic_slice_in_dim(
        early[: 6 * width].reshape(6, width), member * shard_rows, shard_rows, 1
    )
    six = jnp.transpose(six)
    up_total = lax.dynamic_slice_in_dim(early, 6 * width + own_tp * ff_width, ff_width, 0)
    v_total = lax.dynamic_slice_in_dim(
        early, 6 * width + tp_count * ff_width + own_tp * head_width, head_width, 0
    )
    q_total = lax.dynamic_slice_in_dim(q_bias_grad, own_tp * head_width, head_width, 0)
    return (
        output,
        tokens_out,
        qkv_grad.reshape(shard_rows, 3, head_width),
        jnp.stack([q_total, v_total]),
        second_grad[:, :head_width],
        second_grad[:, head_width : head_width + ff_width],
        up_total,
        second_grad[:, head_width + ff_width :],
        six[:, :2],
        six[:, 2:],
    )


def solution(mesh):
    in_specs = (
        P("fsdp", "ctx", None),
        P(("fsdp", "ctx"), None, "tp"),
        P(None, "tp"),
        P(("fsdp", "ctx"), "tp"),
        P(("fsdp", "ctx"), "tp"),
        P("tp"),
        P(("fsdp", "ctx"), "tp"),
        P(("fsdp", "ctx"), None),
        P(("fsdp", "ctx"), None),
        P("fsdp", "ctx", None),
    )
    out_specs = (
        P("fsdp", ("ctx", "tp"), None),
        P("fsdp", ("ctx", "tp"), None),
        P(("fsdp", "ctx"), None, "tp"),
        P(None, "tp"),
        P(("fsdp", "ctx"), "tp"),
        P(("fsdp", "ctx"), "tp"),
        P("tp"),
        P(("fsdp", "ctx"), "tp"),
        P(("fsdp", "ctx"), None),
        P(("fsdp", "ctx"), None),
    )
    return jax.shard_map(body, mesh=mesh, in_specs=in_specs, out_specs=out_specs, check_vma=False)
```

```python
import jax
import jax.numpy as jnp
from jax import lax
from jax.experimental import pallas as pl
from jax.experimental.pallas import tpu as pltpu
from jax.sharding import PartitionSpec as P


HD = 64
B = jnp.bfloat16
F = jnp.float32
epsilon = 1e-12
score_scale = 0.125
LOG2E = 1.4426950408889634
WEIGHT_AXES = ("tp", "fsdp", "ctx")


def dot(left, right, left_dim, right_dim):
    return lax.dot_general(
        left, right, (((left_dim,), (right_dim,)), ((), ())), preferred_element_type=F
    )


def split_low(value, count):
    parts = []
    for _ in range(count):
        part = value.astype(B)
        parts.append(part)
        value = value - part.astype(F)
    return parts


def pick_block(size, wanted):
    while size % wanted:
        wanted //= 2
    return wanted


def forward_kernel(*refs, chunks, first, last, bk):
    q_ref = refs[0]
    kv_refs = refs[1 : 1 + chunks]
    at = 1 + chunks
    if not first:
        o_in, stat_in = refs[at : at + 2]
        at += 2
    o_ref, stat_ref, qx, kx, vx = refs[at:]
    rows = q_ref.shape[-1]
    keys = kx.shape[-1]
    scaled = q_ref[0].astype(F) * (score_scale * LOG2E)
    high, rest = split_low(scaled, 2)
    qx[0:HD, :] = high
    qx[HD : 2 * HD, :] = rest
    size = keys // chunks
    for c, kv_ref in enumerate(kv_refs):
        at = c * size
        kx[0:HD, at : at + size] = kv_ref[0, 0]
        kx[HD : 2 * HD, at : at + size] = kv_ref[0, 0]
        vx[0:HD, at : at + size] = kv_ref[0, 1]
    vx[HD : HD + 16, :] = jnp.ones((16, keys), B)

    def step(i, carry):
        row_max, mixed, total = carry
        off = pl.multiple_of(i * bk, bk)
        scores = dot(kx[:, pl.ds(off, bk)], qx[...], 0, 0)
        new_max = jnp.maximum(row_max, jnp.max(scores, axis=0, keepdims=True))
        probs = jnp.exp2(scores - new_max).astype(B)
        scale = jnp.exp2(row_max - new_max)
        more = dot(vx[:, pl.ds(off, bk)], probs, 1, 0)
        return new_max, mixed * scale + more[0:HD, :], total * scale + more[HD : HD + 1, :]

    if first:
        start = (
            jnp.full((1, rows), -jnp.inf, F),
            jnp.zeros((HD, rows), F),
            jnp.zeros((1, rows), F),
        )
    else:
        start = (stat_in[0, 0, 0:1, :], o_in[0], stat_in[0, 0, 1:2, :])
    row_max, mixed, total = lax.fori_loop(0, keys // bk, step, start)
    if last:
        o_ref[0] = mixed / total
        stat_ref[0, 0] = row_max + jnp.log2(total)
    else:
        o_ref[0] = mixed
        stat_ref[0, 0, 0:1, :] = row_max
        stat_ref[0, 0, 1:2, :] = total


def attention_forward(q_t, kv_list, state, last, bk):
    parts, width, rows = q_t.shape
    chunks = len(kv_list)
    keys = kv_list[0].shape[3]
    heads = width // HD
    bk = pick_block(keys * chunks, bk)
    first = state is None
    row_spec = pl.BlockSpec((1, HD, rows), lambda t, h: (t, h, 0))
    two_spec = pl.BlockSpec((1, 1, 2, rows), lambda t, h: (t, h, 0, 0))
    one_spec = pl.BlockSpec((1, 1, 1, rows), lambda t, h: (t, h, 0, 0))
    key_spec = pl.BlockSpec((1, 2, HD, keys), lambda t, h: (t, 0, h, 0))
    total = parts * heads * rows * keys * chunks
    return pl.pallas_call(
        lambda *refs: forward_kernel(*refs, chunks=chunks, first=first, last=last, bk=bk),
        grid=(parts, heads),
        in_specs=[row_spec] + [key_spec] * chunks + ([] if first else [row_spec, two_spec]),
        out_specs=[row_spec, one_spec if last else two_spec],
        out_shape=[
            jax.ShapeDtypeStruct((parts, width, rows), F),
            jax.ShapeDtypeStruct((parts, heads, 1 if last else 2, rows), F),
        ],
        scratch_shapes=[
            pltpu.VMEM((2 * HD, rows), B),
            pltpu.VMEM((2 * HD, keys * chunks), B),
            pltpu.VMEM((HD + 16, keys * chunks), B),
        ],
        compiler_params=pltpu.CompilerParams(
            vmem_limit_bytes=56 << 20, dimension_semantics=("arbitrary", "arbitrary")
        ),
        cost_estimate=pl.CostEstimate(
            flops=1024 * total, transcendentals=total, bytes_accessed=16 << 20
        ),
        name="attn_forward",
    )(q_t, *kv_list, *(() if first else state))


def backward_kernel(
    q_ref,
    kv_ref,
    do_ref,
    lse_ref,
    delta_ref,
    dq_in,
    dq_ref,
    dkv_ref,
    qx,
    kx,
    dx,
    vx,
    dq_acc,
    *,
    bk,
    bq,
):
    rows = q_ref.shape[-1]
    keys = kv_ref.shape[-1]
    scaled = q_ref[0].astype(F) * (score_scale * LOG2E)
    high, rest = split_low(scaled, 2)
    sub = lax.broadcasted_iota(jnp.int32, (16, rows), 0)

    def stacked(value):
        block = jnp.zeros((16, rows), F)
        for j, part in enumerate(split_low(value, 3)):
            block = jnp.where(sub == j, jnp.broadcast_to(part.astype(F), (16, rows)), block)
        return block.astype(B)

    qx[0:HD, :] = high
    qx[HD : 2 * HD, :] = rest
    qx[2 * HD : 2 * HD + 16, :] = stacked(lse_ref[0, 0])
    dx[0:HD, :] = do_ref[0]
    dx[HD : HD + 16, :] = stacked(delta_ref[0, 0])
    kx[0:HD, :] = kv_ref[0, 0]
    kx[HD : 2 * HD, :] = kv_ref[0, 0]
    kx[2 * HD : 2 * HD + 16, :] = jnp.full((16, keys), -1.0, B)
    vx[0:HD, :] = kv_ref[0, 1]
    vx[HD : HD + 16, :] = jnp.full((16, keys), -1.0, B)
    dq_acc[...] = jnp.zeros_like(dq_acc)

    def step(i, carry):
        off = pl.multiple_of(i * bk, bk)
        k_part = kx[:, pl.ds(off, bk)]
        v_part = vx[:, pl.ds(off, bk)]
        dk_part = jnp.zeros((HD, bk), F)
        dv_part = jnp.zeros((HD, bk), F)
        for j in range(0, rows, bq):
            probs = jnp.exp2(dot(qx[:, j : j + bq], k_part, 0, 0))
            prob_grad = dot(dx[:, j : j + bq], v_part, 0, 0)
            score_low = (probs * prob_grad).astype(B)
            prob_low = probs.astype(B)
            dv_part = dv_part + dot(dx[0:HD, j : j + bq], prob_low, 1, 0)
            dk_part = dk_part + dot(q_ref[0, :, j : j + bq], score_low, 1, 0)
            dq_acc[j : j + bq, :] += dot(score_low, k_part[0:HD, :], 1, 1)
        dkv_ref[0, 0, :, pl.ds(off, bk)] = (dk_part * score_scale).astype(B)
        dkv_ref[0, 1, :, pl.ds(off, bk)] = dv_part.astype(B)
        return carry

    lax.fori_loop(0, keys // bk, step, 0)
    dq_ref[0] = dq_in[0] + jnp.transpose(dq_acc[...] * score_scale)


def attention_backward(q_t, kv_t, do_t, lse, delta, dq_t, bk, bq):
    parts, width, rows = q_t.shape
    keys = kv_t.shape[3]
    heads = width // HD
    bk = pick_block(keys, bk)
    bq = pick_block(rows, bq)
    total = parts * heads * rows * keys
    row_spec = pl.BlockSpec((1, HD, rows), lambda t, h: (t, h, 0))
    stat_spec = pl.BlockSpec((1, 1, 1, rows), lambda t, h: (t, h, 0, 0))
    key_spec = pl.BlockSpec((1, 2, HD, keys), lambda t, h: (t, 0, h, 0))
    return pl.pallas_call(
        lambda *refs: backward_kernel(*refs, bk=bk, bq=bq),
        grid=(parts, heads),
        in_specs=[row_spec, key_spec, row_spec, stat_spec, stat_spec, row_spec],
        out_specs=[row_spec, key_spec],
        out_shape=[
            jax.ShapeDtypeStruct((parts, width, rows), F),
            jax.ShapeDtypeStruct((parts, 2, width, keys), B),
        ],
        scratch_shapes=[
            pltpu.VMEM((2 * HD + 16, rows), B),
            pltpu.VMEM((2 * HD + 16, keys), B),
            pltpu.VMEM((HD + 16, rows), B),
            pltpu.VMEM((HD + 16, keys), B),
            pltpu.VMEM((rows, HD), F),
        ],
        compiler_params=pltpu.CompilerParams(
            vmem_limit_bytes=56 << 20, dimension_semantics=("arbitrary", "arbitrary")
        ),
        cost_estimate=pl.CostEstimate(
            flops=2048 * total, transcendentals=total, bytes_accessed=16 << 20
        ),
        input_output_aliases={5: 0},
        name="attn_backward",
    )(q_t, kv_t, do_t, lse, delta, dq_t)


def ring_gather(block):
    count = lax.axis_size("ctx")
    up = [(i, (i + 1) % count) for i in range(count)]
    down = [((i + 1) % count, i) for i in range(count)]
    half = block.shape[0] // 2
    first, second = block[:half], block[half:]
    pieces = []
    for _ in range(1, count):
        first = lax.ppermute(first, "ctx", up)
        second = lax.ppermute(second, "ctx", down)
        pieces.append((first, second))
    return pieces


def ring_return(first, second):
    count = lax.axis_size("ctx")
    up = [(i, (i + 1) % count) for i in range(count)]
    down = [((i + 1) % count, i) for i in range(count)]
    return lax.ppermute(first, "ctx", down), lax.ppermute(second, "ctx", up)


def scatter_sum(blocks, order):
    sizes = {axis: lax.axis_size(axis) for axis in WEIGHT_AXES}
    bits = []
    for axis in WEIGHT_AXES:
        bit = sizes[axis] // 2
        while bit:
            bits.append((axis, bit))
            bit //= 2
    left = blocks.reshape((2,) * len(bits) + blocks.shape[2:])
    todo = sorted(
        bits,
        key=lambda one: (one != ("fsdp", 1), order.index(one[0]), -one[1]),
    )
    for axis, bit in todo:
        dim = bits.index((axis, bit))
        bits.remove((axis, bit))
        mine = (lax.axis_index(axis) // bit) % 2
        sent = lax.dynamic_index_in_dim(left, 1 - mine, dim, keepdims=False)
        kept = lax.dynamic_index_in_dim(left, mine, dim, keepdims=False)
        got = lax.ppermute(sent, axis, [(i, i ^ bit) for i in range(sizes[axis])])
        total = kept.astype(F) + got.astype(F)
        left = total.astype(B) if bits else total
    return left


def sum_all(vector):
    for axis in ("fsdp", "tp", "ctx"):
        size = lax.axis_size(axis)
        bit = 1
        while bit < size:
            vector = vector + lax.ppermute(vector, axis, [(i, i ^ bit) for i in range(size)])
            bit *= 2
    return vector


def tp_gather(vector):
    size = lax.axis_size("tp")
    own = lax.axis_index("tp")
    out = jnp.zeros((size,) + vector.shape, vector.dtype)
    out = lax.dynamic_update_index_in_dim(out, vector, own, 0)
    for shift in range(1, size):
        got = lax.ppermute(vector, "tp", [(i, (i + shift) % size) for i in range(size)])
        out = lax.dynamic_update_index_in_dim(out, got, (own - shift) % size, 0)
    return out


def tp_exchange(rows):
    size = lax.axis_size("tp")
    own = lax.axis_index("tp")
    seqs, length, width = rows.shape
    split = rows.reshape(seqs, size, length // size, width)
    out = jnp.zeros((size, seqs, length // size, width), rows.dtype)
    kept = lax.dynamic_index_in_dim(split, own, 1, keepdims=False)
    out = lax.dynamic_update_index_in_dim(out, kept, own, 0)
    for shift in range(1, size):
        sent = lax.dynamic_index_in_dim(split, (own + shift) % size, 1, keepdims=False)
        got = lax.ppermute(sent, "tp", [(i, (i + shift) % size) for i in range(size)])
        out = lax.dynamic_update_index_in_dim(out, got, (own - shift) % size, 0)
    return out.reshape(size * seqs, length // size, width)


def norm_forward(hidden, gain, shift):
    center = hidden - jnp.mean(hidden, axis=-1, keepdims=True)
    inv_scale = lax.rsqrt(jnp.mean(center * center, axis=-1, keepdims=True) + epsilon)
    normed = center * inv_scale
    return (normed * gain + shift, normed, inv_scale)


def norm_backward(grad_out, normed, inv_scale, gain):
    grad_norm = grad_out * gain
    return inv_scale * (
        grad_norm
        - jnp.mean(grad_norm, axis=-1, keepdims=True)
        - normed * jnp.mean(grad_norm * normed, axis=-1, keepdims=True)
    )


def gelu_exact(values):
    return jax.nn.gelu(values, approximate=False)


def layer(
    tokens,
    qkv_weight,
    qv_bias,
    out_weight,
    up_weight,
    up_bias,
    down_weight,
    norm_gains,
    row_biases,
    cotangent,
):
    seq_count, local_len, width = tokens.shape
    tp_count = lax.axis_size("tp")
    own_seqs = seq_count // tp_count
    first_seq = lax.axis_index("tp") * own_seqs
    own_tokens = lax.dynamic_slice_in_dim(tokens, first_seq, own_seqs, 0)
    own_cotangent = lax.dynamic_slice_in_dim(cotangent, first_seq, own_seqs, 0)
    rows = own_seqs * local_len
    x_own = own_tokens.reshape(rows, width)
    shard_rows = qkv_weight.shape[0]
    head_width = qkv_weight.shape[2]
    ff_width = up_weight.shape[1]
    pad = 128 - norm_gains.shape[1] - row_biases.shape[1]

    first_shard = jnp.concatenate(
        [
            qkv_weight.reshape(shard_rows, 3 * head_width),
            norm_gains,
            row_biases,
            jnp.zeros((shard_rows, pad), B),
        ],
        axis=1,
    )
    first_all = lax.all_gather(first_shard, WEIGHT_AXES, axis=0, tiled=True)
    first_all = first_all.reshape(tp_count, width, first_shard.shape[1])
    x_pieces = [ring_gather(own_tokens[s]) for s in range(own_seqs)]
    second_shard = jnp.concatenate([out_weight, up_weight, down_weight], axis=1)
    second_all = lax.all_gather(second_shard, WEIGHT_AXES, axis=0, tiled=True)
    second_all = second_all.reshape(tp_count, width, second_shard.shape[1])
    w_q = first_all[:, :, :head_width]
    w_kv = first_all[:, :, head_width : 3 * head_width]
    rows_all = jnp.transpose(first_all[0, :, 3 * head_width :]).astype(F)
    gain1, gain2 = rows_all[0], rows_all[1]
    out_bias, shift1, down_bias, shift2 = (rows_all[2 + i] for i in range(4))
    w_out = second_all[:, :, :head_width]
    w_up = second_all[:, :, head_width : head_width + ff_width]
    w_down = second_all[:, :, head_width + ff_width :]
    bias_all = tp_gather(jnp.concatenate([qv_bias.reshape(-1), up_bias]))
    q_bias = bias_all[:, :head_width].astype(F)
    v_bias = bias_all[:, head_width : 2 * head_width].astype(F)
    u_bias = bias_all[:, 2 * head_width :].astype(F)
    kv_bias = jnp.concatenate([jnp.zeros_like(v_bias), v_bias], axis=1)

    def project(block):
        got = (dot(w_kv, block, 1, 1) + kv_bias[:, :, None]).astype(B)
        return got.reshape(tp_count, 2, head_width, block.shape[0])

    x_chunks = [
        [own_tokens[s]] + [jnp.concatenate(pair, axis=0) for pair in x_pieces[s]]
        for s in range(own_seqs)
    ]
    chunk_count = len(x_chunks[0])
    near = (chunk_count + 1) // 2
    q_t, kv_t, om_t, lse = [], [], [], []
    for s in range(own_seqs):
        q_s = (dot(w_q, own_tokens[s], 1, 1) + q_bias[:, :, None]).astype(B)
        kv_s = [project(block) for block in x_chunks[s][:near]]
        if near < chunk_count:
            state = attention_forward(q_s, kv_s, None, False, 2048)
            kv_far = [project(block) for block in x_chunks[s][near:]]
            done = attention_forward(q_s, kv_far, state, True, 2048)
            kv_s = kv_s + kv_far
        else:
            done = attention_forward(q_s, kv_s, None, True, 2048)
        q_t.append(q_s)
        kv_t.append(kv_s)
        om_t.append(done[0])
        lse.append(done[1])
    mixed_t = jnp.concatenate([one.astype(B) for one in om_t], axis=2)
    attn_part = sum(dot(mixed_t[t], w_out[t], 0, 1) for t in range(tp_count))
    x_float = x_own.astype(F)
    first_out, first_norm, first_scale = norm_forward(
        x_float + attn_part + out_bias, gain1, shift1
    )
    first_low = first_out.astype(B)

    act_low, gelu_back = [], []
    for t in range(tp_count):
        inner = dot(first_low, w_up[t], 1, 0) + u_bias[t]
        activated, back = jax.vjp(gelu_exact, inner)
        act_low.append(activated.astype(B))
        gelu_back.append(back)
    ffn_out = sum(dot(act_low[t], w_down[t], 1, 1) for t in range(tp_count)) + down_bias
    grad_final = own_cotangent.reshape(rows, width).astype(F)
    final_out, final_norm, final_scale = norm_forward(first_out + ffn_out, gain2, shift2)
    output = tp_exchange(final_out.astype(B).reshape(own_seqs, local_len, width))
    gain2_grad = jnp.sum(grad_final * final_norm, axis=0)
    shift2_grad = jnp.sum(grad_final, axis=0)
    grad_second = norm_backward(grad_final, final_norm, final_scale, gain2)
    df = grad_second.astype(B)
    down_bias_grad = jnp.sum(df.astype(F), axis=0)
    inner_low = [
        gelu_back[t](dot(df, w_down[t], 1, 0))[0].astype(B) for t in range(tp_count)
    ]
    up_bias_grad = [jnp.sum(inner_low[t].astype(F), axis=0) for t in range(tp_count)]
    first_grad = grad_second + sum(dot(inner_low[t], w_up[t], 1, 1) for t in range(tp_count))
    gain1_grad = jnp.sum(first_grad * first_norm, axis=0)
    shift1_grad = jnp.sum(first_grad, axis=0)
    resid_grad = norm_backward(first_grad, first_norm, first_scale, gain1)
    da = resid_grad.astype(B)
    out_bias_grad = jnp.sum(da.astype(F), axis=0)
    second_grad = jnp.stack(
        [
            jnp.concatenate(
                [
                    dot(da, mixed_t[t], 0, 1).astype(B),
                    dot(first_low, inner_low[t], 0, 0).astype(B),
                    dot(df, act_low[t], 0, 0).astype(B),
                ],
                axis=1,
            )
            for t in range(tp_count)
        ]
    )
    do_t = dot(w_out, da, 1, 1).astype(B)
    do_t, second_grad = lax.optimization_barrier((do_t, second_grad))
    second_grad = lax.psum_scatter(
        second_grad.reshape(tp_count * width, second_shard.shape[1]),
        WEIGHT_AXES,
        scatter_dimension=0,
        tiled=True,
    ).astype(F)

    v_bias_grad = jnp.sum(do_t.astype(F), axis=2)
    early = sum_all(
        jnp.concatenate(
            [gain1_grad, gain2_grad, out_bias_grad, shift1_grad, down_bias_grad, shift2_grad]
            + up_bias_grad
            + [v_bias_grad.reshape(-1)]
        )
    )
    kv_grad = [0.0] * tp_count
    q_grad = [0.0] * tp_count
    q_bias_grad = 0.0
    own_grads = []
    half = local_len // 2
    for s in range(own_seqs):
        do_s = do_t[:, :, s * local_len : (s + 1) * local_len]
        delta = (om_t[s] * do_s.astype(F)).reshape(tp_count, head_width // HD, HD, local_len)
        delta = jnp.sum(delta, axis=2, keepdims=True)
        dq = jnp.zeros(om_t[s].shape, F)
        got = None
        for c in reversed(range(chunk_count)):
            dq, dkv = attention_backward(
                q_t[s], kv_t[s][c], do_s, lse[s], delta, dq, 1024, 512
            )
            dkv = dkv.reshape(tp_count, 2 * head_width, dkv.shape[3])
            part = sum(dot(dkv[t], w_kv[t], 0, 1) for t in range(tp_count))
            kv_grad = [kv_grad[t] + dot(x_chunks[s][c], dkv[t], 0, 1) for t in range(tp_count)]
            if c:
                one, two = part[:half], part[half:]
                if got is not None:
                    one = one + got[0].astype(F)
                    two = two + got[1].astype(F)
                one, two, dq, *kv_grad = lax.optimization_barrier(
                    (one.astype(B), two.astype(B), dq, *kv_grad)
                )
                got = ring_return(one, two)
        dq_low = dq.astype(B)
        q_bias_grad = q_bias_grad + jnp.sum(dq_low.astype(F), axis=2)
        q_grad = [q_grad[t] + dot(own_tokens[s], dq_low[t], 0, 1) for t in range(tp_count)]
        part = part + sum(dot(dq_low[t], w_q[t], 0, 1) for t in range(tp_count))
        if got is not None:
            part = part + jnp.concatenate(got, axis=0).astype(F)
        own_grads.append(part)
    q_bias_grad = sum_all(q_bias_grad.reshape(-1))
    qkv_grad = jnp.stack(
        [jnp.concatenate([q_grad[t], kv_grad[t]], axis=1).astype(B) for t in range(tp_count)]
    )
    qkv_grad = qkv_grad.reshape(tp_count, width // shard_rows, shard_rows, 3 * head_width)
    cut = (3 * head_width // 256) * 128
    qkv_grad = jnp.concatenate(
        [
            scatter_sum(qkv_grad[..., :cut], ("tp", "fsdp", "ctx")),
            scatter_sum(qkv_grad[..., cut:], ("fsdp", "tp", "ctx")),
        ],
        axis=1,
    )
    tokens_grad = resid_grad.reshape(own_seqs, local_len, width) + jnp.stack(own_grads)
    tokens_out = tp_exchange(tokens_grad.astype(B))

    member = lax.axis_index("fsdp") * lax.axis_size("ctx") + lax.axis_index("ctx")
    own_tp = lax.axis_index("tp")
    six = lax.dynamic_slice_in_dim(
        early[: 6 * width].reshape(6, width), member * shard_rows, shard_rows, 1
    )
    six = jnp.transpose(six)
    up_total = lax.dynamic_slice_in_dim(early, 6 * width + own_tp * ff_width, ff_width, 0)
    v_total = lax.dynamic_slice_in_dim(
        early, 6 * width + tp_count * ff_width + own_tp * head_width, head_width, 0
    )
    q_total = lax.dynamic_slice_in_dim(q_bias_grad, own_tp * head_width, head_width, 0)
    return (
        output,
        tokens_out,
        qkv_grad.reshape(shard_rows, 3, head_width),
        jnp.stack([q_total, v_total]),
        second_grad[:, :head_width],
        second_grad[:, head_width : head_width + ff_width],
        up_total,
        second_grad[:, head_width + ff_width :],
        six[:, :2],
        six[:, 2:],
    )


def solution(mesh):
    in_specs = (
        P("fsdp", "ctx", None),
        P(("fsdp", "ctx"), None, "tp"),
        P(None, "tp"),
        P(("fsdp", "ctx"), "tp"),
        P(("fsdp", "ctx"), "tp"),
        P("tp"),
        P(("fsdp", "ctx"), "tp"),
        P(("fsdp", "ctx"), None),
        P(("fsdp", "ctx"), None),
        P("fsdp", "ctx", None),
    )
    out_specs = (
        P("fsdp", ("ctx", "tp"), None),
        P("fsdp", ("ctx", "tp"), None),
        P(("fsdp", "ctx"), None, "tp"),
        P(None, "tp"),
        P(("fsdp", "ctx"), "tp"),
        P(("fsdp", "ctx"), "tp"),
        P("tp"),
        P(("fsdp", "ctx"), "tp"),
        P(("fsdp", "ctx"), None),
        P(("fsdp", "ctx"), None),
    )
    return jax.shard_map(layer, mesh=mesh, in_specs=in_specs, out_specs=out_specs, check_vma=False)
```

```python
import jax
import jax.numpy as jnp
from jax import lax
from jax.experimental import pallas as pl
from jax.experimental.pallas import tpu as pltpu
from jax.sharding import PartitionSpec as P


HD = 64
B = jnp.bfloat16
F = jnp.float32
epsilon = 1e-12
score_scale = 0.125
LOG2E = 1.4426950408889634
WEIGHT_AXES = ("tp", "fsdp", "ctx")


def dot(left, right, left_dim, right_dim):
    return lax.dot_general(
        left, right, (((left_dim,), (right_dim,)), ((), ())), preferred_element_type=F
    )


def split_low(value, count):
    parts = []
    for _ in range(count):
        part = value.astype(B)
        parts.append(part)
        value = value - part.astype(F)
    return parts


def pick_block(size, wanted):
    while size % wanted:
        wanted //= 2
    return wanted


def forward_kernel(*refs, chunks, first, last, bk):
    q_ref = refs[0]
    kv_refs = refs[1 : 1 + chunks]
    at = 1 + chunks
    if not first:
        o_in, stat_in = refs[at : at + 2]
        at += 2
    o_ref, stat_ref = refs[at : at + 2]
    qx, kx, vx = refs[-3:]
    rows = q_ref.shape[-1]
    keys = kx.shape[-1]
    scaled = q_ref[0].astype(F) * (score_scale * LOG2E)
    high, rest = split_low(scaled, 2)
    qx[0:HD, :] = high
    qx[HD : 2 * HD, :] = rest
    size = keys // chunks
    for c, kv_ref in enumerate(kv_refs):
        at = c * size
        kx[0:HD, at : at + size] = kv_ref[0, 0]
        kx[HD : 2 * HD, at : at + size] = kv_ref[0, 0]
        vx[0:HD, at : at + size] = kv_ref[0, 1]
    vx[HD : HD + 16, :] = jnp.ones((16, keys), B)

    def step(i, carry):
        row_max, mixed, total = carry
        off = pl.multiple_of(i * bk, bk)
        scores = dot(kx[:, pl.ds(off, bk)], qx[...], 0, 0)
        new_max = jnp.maximum(row_max, jnp.max(scores, axis=0, keepdims=True))
        probs = jnp.exp2(scores - new_max).astype(B)
        scale = jnp.exp2(row_max - new_max)
        more = dot(vx[:, pl.ds(off, bk)], probs, 1, 0)
        return new_max, mixed * scale + more[0:HD, :], total * scale + more[HD : HD + 1, :]

    if first:
        start = (
            jnp.full((1, rows), -jnp.inf, F),
            jnp.zeros((HD, rows), F),
            jnp.zeros((1, rows), F),
        )
    else:
        start = (stat_in[0, 0, 0:1, :], o_in[0], stat_in[0, 0, 1:2, :])
    row_max, mixed, total = lax.fori_loop(0, keys // bk, step, start)
    if last:
        mixed = mixed / total
        o_ref[0] = mixed
        refs[-4][0] = mixed.astype(B)
        stat_ref[0, 0] = row_max + jnp.log2(total)
    else:
        o_ref[0] = mixed
        stat_ref[0, 0, 0:1, :] = row_max
        stat_ref[0, 0, 1:2, :] = total


def attention_forward(q_t, kv_list, state, last, bk):
    parts, width, rows = q_t.shape
    chunks = len(kv_list)
    keys = kv_list[0].shape[3]
    heads = width // HD
    bk = pick_block(keys * chunks, bk)
    first = state is None
    row_spec = pl.BlockSpec((1, HD, rows), lambda t, h: (t, h, 0))
    two_spec = pl.BlockSpec((1, 1, 2, rows), lambda t, h: (t, h, 0, 0))
    one_spec = pl.BlockSpec((1, 1, 1, rows), lambda t, h: (t, h, 0, 0))
    key_spec = pl.BlockSpec((1, 2, HD, keys), lambda t, h: (t, 0, h, 0))
    total = parts * heads * rows * keys * chunks
    return pl.pallas_call(
        lambda *refs: forward_kernel(*refs, chunks=chunks, first=first, last=last, bk=bk),
        grid=(parts, heads),
        in_specs=[row_spec] + [key_spec] * chunks + ([] if first else [row_spec, two_spec]),
        out_specs=[row_spec, one_spec, row_spec] if last else [row_spec, two_spec],
        out_shape=[
            jax.ShapeDtypeStruct((parts, width, rows), F),
            jax.ShapeDtypeStruct((parts, heads, 1 if last else 2, rows), F),
        ]
        + ([jax.ShapeDtypeStruct((parts, width, rows), B)] if last else []),
        scratch_shapes=[
            pltpu.VMEM((2 * HD, rows), B),
            pltpu.VMEM((2 * HD, keys * chunks), B),
            pltpu.VMEM((HD + 16, keys * chunks), B),
        ],
        compiler_params=pltpu.CompilerParams(
            vmem_limit_bytes=56 << 20, dimension_semantics=("arbitrary", "arbitrary")
        ),
        cost_estimate=pl.CostEstimate(
            flops=1024 * total, transcendentals=total, bytes_accessed=16 << 20
        ),
        name="attn_forward",
    )(q_t, *kv_list, *(() if first else state))


def backward_kernel(*refs, first, bk, bq):
    q_ref, kv_ref, do_ref, lse_ref, om_ref = refs[:5]
    dq_ref, dkv_ref, qx, kx, dx, vx, dq_acc = refs[-7:]
    rows = q_ref.shape[-1]
    keys = kv_ref.shape[-1]
    scaled = q_ref[0].astype(F) * (score_scale * LOG2E)
    high, rest = split_low(scaled, 2)
    sub = lax.broadcasted_iota(jnp.int32, (16, rows), 0)

    def stacked(value):
        block = jnp.zeros((16, rows), F)
        for j, part in enumerate(split_low(value, 3)):
            block = jnp.where(sub == j, jnp.broadcast_to(part.astype(F), (16, rows)), block)
        return block.astype(B)

    qx[0:HD, :] = high
    qx[HD : 2 * HD, :] = rest
    qx[2 * HD : 2 * HD + 16, :] = stacked(lse_ref[0, 0])
    dx[0:HD, :] = do_ref[0]
    delta = jnp.sum(om_ref[0] * do_ref[0].astype(F), axis=0, keepdims=True)
    dx[HD : HD + 16, :] = stacked(delta)
    kx[0:HD, :] = kv_ref[0, 0]
    kx[HD : 2 * HD, :] = kv_ref[0, 0]
    kx[2 * HD : 2 * HD + 16, :] = jnp.full((16, keys), -1.0, B)
    vx[0:HD, :] = kv_ref[0, 1]
    vx[HD : HD + 16, :] = jnp.full((16, keys), -1.0, B)
    dq_acc[...] = jnp.zeros_like(dq_acc)

    def step(i, carry):
        off = pl.multiple_of(i * bk, bk)
        k_part = kx[:, pl.ds(off, bk)]
        v_part = vx[:, pl.ds(off, bk)]
        dk_part = jnp.zeros((HD, bk), F)
        dv_part = jnp.zeros((HD, bk), F)
        for j in range(0, rows, bq):
            probs = jnp.exp2(dot(qx[:, j : j + bq], k_part, 0, 0))
            prob_grad = dot(dx[:, j : j + bq], v_part, 0, 0)
            score_low = (probs * prob_grad).astype(B)
            prob_low = probs.astype(B)
            dv_part = dv_part + dot(dx[0:HD, j : j + bq], prob_low, 1, 0)
            dk_part = dk_part + dot(q_ref[0, :, j : j + bq], score_low, 1, 0)
            dq_acc[j : j + bq, :] += dot(score_low, k_part[0:HD, :], 1, 1)
        dkv_ref[0, 0, :, pl.ds(off, bk)] = (dk_part * score_scale).astype(B)
        dkv_ref[0, 1, :, pl.ds(off, bk)] = dv_part.astype(B)
        return carry

    lax.fori_loop(0, keys // bk, step, 0)
    total = jnp.transpose(dq_acc[...] * score_scale)
    if not first:
        total = total + refs[5][0]
    dq_ref[0] = total.astype(dq_ref.dtype)


def attention_backward(q_t, kv_t, do_t, lse, om_t, dq_t, last, bk, bq):
    parts, width, rows = q_t.shape
    keys = kv_t.shape[3]
    heads = width // HD
    bk = pick_block(keys, bk)
    bq = pick_block(rows, bq)
    first = dq_t is None
    total = parts * heads * rows * keys
    row_spec = pl.BlockSpec((1, HD, rows), lambda t, h: (t, h, 0))
    stat_spec = pl.BlockSpec((1, 1, 1, rows), lambda t, h: (t, h, 0, 0))
    key_spec = pl.BlockSpec((1, 2, HD, keys), lambda t, h: (t, 0, h, 0))
    return pl.pallas_call(
        lambda *refs: backward_kernel(*refs, first=first, bk=bk, bq=bq),
        grid=(parts, heads),
        in_specs=[row_spec, key_spec, row_spec, stat_spec, row_spec]
        + ([] if first else [row_spec]),
        out_specs=[row_spec, key_spec],
        out_shape=[
            jax.ShapeDtypeStruct((parts, width, rows), B if last else F),
            jax.ShapeDtypeStruct((parts, 2, width, keys), B),
        ],
        scratch_shapes=[
            pltpu.VMEM((2 * HD + 16, rows), B),
            pltpu.VMEM((2 * HD + 16, keys), B),
            pltpu.VMEM((HD + 16, rows), B),
            pltpu.VMEM((HD + 16, keys), B),
            pltpu.VMEM((rows, HD), F),
        ],
        compiler_params=pltpu.CompilerParams(
            vmem_limit_bytes=56 << 20, dimension_semantics=("arbitrary", "arbitrary")
        ),
        cost_estimate=pl.CostEstimate(
            flops=2048 * total, transcendentals=total, bytes_accessed=16 << 20
        ),
        name="attn_backward",
    )(q_t, kv_t, do_t, lse, om_t, *([] if first else [dq_t]))


def gelu_both(u):
    z = jnp.abs(u) * 0.7071067811865476
    t = 1.0 / (1.0 + 0.5 * z)
    series = 0.17087277
    for c in (
        -0.82215223,
        1.48851587,
        -1.13520398,
        0.27886807,
        -0.18628806,
        0.09678418,
        0.37409196,
        1.00002368,
        -1.26551223,
    ):
        series = series * t + c
    bell = jnp.exp(u * u * -0.5)
    tail = (0.5 * t) * bell * jnp.exp(series)
    below = jnp.where(u >= 0, 1.0 - tail, tail)
    return u * below, below + u * (bell * 0.3989422804014327)


def ffn_forward_kernel(y_ref, up_ref, down_ref, bias_ref, act_ref, slope_ref, out_ref, *, br):
    start = (pl.program_id(0) == 0) & (pl.program_id(1) == 0)

    @pl.when(start)
    def _():
        out_ref[...] = jnp.zeros_like(out_ref)

    for r in range(0, y_ref.shape[0], br):
        u = dot(y_ref[r : r + br, :], up_ref[0], 1, 0) + bias_ref[...]
        act, slope = gelu_both(u)
        low = act.astype(B)
        act_ref[r : r + br, :] = low
        slope_ref[r : r + br, :] = slope
        out_ref[r : r + br, :] += dot(low, down_ref[0], 1, 1)


def ffn_backward_kernel(df_ref, up_ref, down_ref, slope_ref, du_ref, sum_ref, out_ref, *, br):
    start = (pl.program_id(0) == 0) & (pl.program_id(1) == 0)

    @pl.when(start)
    def _():
        out_ref[...] = jnp.zeros_like(out_ref)

    total = jnp.zeros(sum_ref.shape, F)
    for r in range(0, df_ref.shape[0], br):
        du = (dot(df_ref[r : r + br, :], down_ref[0], 1, 0) * slope_ref[r : r + br, :]).astype(B)
        du_ref[r : r + br, :] = du
        total = total + jnp.sum(du.astype(F), axis=0, keepdims=True)
        out_ref[r : r + br, :] += dot(du, up_ref[0], 1, 1)
    sum_ref[...] = total


def ffn_specs(rows, width, weights, head_width, ff_width):
    block = head_width
    per = ff_width // block
    up_spec = pl.BlockSpec((1, width, block), lambda t, j: (t, 0, 1 + j))
    down_spec = pl.BlockSpec((1, width, block), lambda t, j: (t, 0, 1 + per + j))
    row_spec = pl.BlockSpec((rows, width), lambda t, j: (0, 0))
    hidden_spec = pl.BlockSpec((rows, block), lambda t, j: (0, t * per + j))
    vector_spec = pl.BlockSpec((1, block), lambda t, j: (0, t * per + j))
    return (weights.shape[0], per), up_spec, down_spec, row_spec, hidden_spec, vector_spec


FFN_PARAMS = pltpu.CompilerParams(
    vmem_limit_bytes=56 << 20, dimension_semantics=("arbitrary", "arbitrary")
)


def ffn_forward(y_low, weights, bias, head_width, ff_width):
    rows, width = y_low.shape
    grid, up_spec, down_spec, row_spec, hidden_spec, vector_spec = ffn_specs(
        rows, width, weights, head_width, ff_width
    )
    hidden = grid[0] * ff_width
    return pl.pallas_call(
        lambda *refs: ffn_forward_kernel(*refs, br=pick_block(rows, 256)),
        grid=grid,
        in_specs=[row_spec, up_spec, down_spec, vector_spec],
        out_specs=[hidden_spec, hidden_spec, row_spec],
        out_shape=[
            jax.ShapeDtypeStruct((rows, hidden), B),
            jax.ShapeDtypeStruct((rows, hidden), F),
            jax.ShapeDtypeStruct((rows, width), F),
        ],
        compiler_params=FFN_PARAMS,
        name="ffn_forward",
    )(y_low, weights, weights, bias)


def ffn_backward(df, weights, slope, head_width, ff_width):
    rows, width = df.shape
    grid, up_spec, down_spec, row_spec, hidden_spec, vector_spec = ffn_specs(
        rows, width, weights, head_width, ff_width
    )
    hidden = grid[0] * ff_width
    return pl.pallas_call(
        lambda *refs: ffn_backward_kernel(*refs, br=pick_block(rows, 256)),
        grid=grid,
        in_specs=[row_spec, up_spec, down_spec, hidden_spec],
        out_specs=[hidden_spec, vector_spec, row_spec],
        out_shape=[
            jax.ShapeDtypeStruct((rows, hidden), B),
            jax.ShapeDtypeStruct((1, hidden), F),
            jax.ShapeDtypeStruct((rows, width), F),
        ],
        compiler_params=FFN_PARAMS,
        name="ffn_backward",
    )(df, weights, weights, slope)


def weight_grad_kernel(da_ref, y_ref, df_ref, mixed_ref, du_ref, act_ref, out_ref, *, per):
    j = pl.program_id(1)

    @pl.when(j == 0)
    def _():
        out_ref[0] = dot(da_ref[...], mixed_ref[0], 0, 1).astype(B)

    @pl.when((j > 0) & (j <= per))
    def _():
        out_ref[0] = dot(y_ref[...], du_ref[...], 0, 0).astype(B)

    @pl.when(j > per)
    def _():
        out_ref[0] = dot(df_ref[...], act_ref[...], 0, 0).astype(B)


def weight_grads(da, y_low, df, mixed_t, du, act):
    rows, width = da.shape
    parts, block, _ = mixed_t.shape
    per = du.shape[1] // parts // block
    row_spec = pl.BlockSpec((rows, width), lambda t, j: (0, 0))
    return pl.pallas_call(
        lambda *refs: weight_grad_kernel(*refs, per=per),
        grid=(parts, 1 + 2 * per),
        in_specs=[
            row_spec,
            row_spec,
            row_spec,
            pl.BlockSpec((1, block, rows), lambda t, j: (t, 0, 0)),
            pl.BlockSpec((rows, block), lambda t, j: (0, t * per + jnp.clip(j - 1, 0, per - 1))),
            pl.BlockSpec(
                (rows, block), lambda t, j: (0, t * per + jnp.clip(j - 1 - per, 0, per - 1))
            ),
        ],
        out_specs=pl.BlockSpec((1, width, block), lambda t, j: (t, 0, j)),
        out_shape=jax.ShapeDtypeStruct((parts, width, block * (1 + 2 * per)), B),
        compiler_params=FFN_PARAMS,
        name="weight_grads",
    )(da, y_low, df, mixed_t, du, act)


def ring_gather(block):
    count = lax.axis_size("ctx")
    up = [(i, (i + 1) % count) for i in range(count)]
    down = [((i + 1) % count, i) for i in range(count)]
    half = block.shape[0] // 2
    first, second = block[:half], block[half:]
    pieces = []
    for _ in range(1, count):
        first = lax.ppermute(first, "ctx", up)
        second = lax.ppermute(second, "ctx", down)
        pieces.append((first, second))
    return pieces


def ring_return(first, second):
    count = lax.axis_size("ctx")
    up = [(i, (i + 1) % count) for i in range(count)]
    down = [((i + 1) % count, i) for i in range(count)]
    return lax.ppermute(first, "ctx", down), lax.ppermute(second, "ctx", up)


def scatter_sum(blocks, order):
    sizes = {axis: lax.axis_size(axis) for axis in WEIGHT_AXES}
    bits = []
    for axis in WEIGHT_AXES:
        bit = sizes[axis] // 2
        while bit:
            bits.append((axis, bit))
            bit //= 2
    left = blocks.reshape((2,) * len(bits) + blocks.shape[2:])
    todo = sorted(
        bits,
        key=lambda one: (one != ("fsdp", 1), order.index(one[0]), -one[1]),
    )
    for axis, bit in todo:
        dim = bits.index((axis, bit))
        bits.remove((axis, bit))
        mine = (lax.axis_index(axis) // bit) % 2
        sent = lax.dynamic_index_in_dim(left, 1 - mine, dim, keepdims=False)
        kept = lax.dynamic_index_in_dim(left, mine, dim, keepdims=False)
        got = lax.ppermute(sent, axis, [(i, i ^ bit) for i in range(sizes[axis])])
        total = kept.astype(F) + got.astype(F)
        left = total.astype(B) if bits else total
    return left


def sum_all(vector):
    every = lax.all_gather(vector.reshape(-1, 128), ("fsdp", "ctx", "tp"), axis=0)
    return jnp.sum(every, axis=0).reshape(-1)


def tp_gather(vector):
    size = lax.axis_size("tp")
    own = lax.axis_index("tp")
    out = jnp.zeros((size,) + vector.shape, vector.dtype)
    out = lax.dynamic_update_index_in_dim(out, vector, own, 0)
    for shift in range(1, size):
        got = lax.ppermute(vector, "tp", [(i, (i + shift) % size) for i in range(size)])
        out = lax.dynamic_update_index_in_dim(out, got, (own - shift) % size, 0)
    return out


def tp_exchange(rows):
    size = lax.axis_size("tp")
    own = lax.axis_index("tp")
    seqs, length, width = rows.shape
    split = rows.reshape(seqs, size, length // size, width)
    out = jnp.zeros((size, seqs, length // size, width), rows.dtype)
    kept = lax.dynamic_index_in_dim(split, own, 1, keepdims=False)
    out = lax.dynamic_update_index_in_dim(out, kept, own, 0)
    for shift in range(1, size):
        sent = lax.dynamic_index_in_dim(split, (own + shift) % size, 1, keepdims=False)
        got = lax.ppermute(sent, "tp", [(i, (i + shift) % size) for i in range(size)])
        out = lax.dynamic_update_index_in_dim(out, got, (own - shift) % size, 0)
    return out.reshape(size * seqs, length // size, width)


def norm_forward(hidden, gain, shift):
    center = hidden - jnp.mean(hidden, axis=-1, keepdims=True)
    inv_scale = lax.rsqrt(jnp.mean(center * center, axis=-1, keepdims=True) + epsilon)
    normed = center * inv_scale
    return (normed * gain + shift, normed, inv_scale)


def norm_backward(grad_out, normed, inv_scale, gain):
    grad_norm = grad_out * gain
    return inv_scale * (
        grad_norm
        - jnp.mean(grad_norm, axis=-1, keepdims=True)
        - normed * jnp.mean(grad_norm * normed, axis=-1, keepdims=True)
    )


def layer(
    tokens,
    qkv_weight,
    qv_bias,
    out_weight,
    up_weight,
    up_bias,
    down_weight,
    norm_gains,
    row_biases,
    cotangent,
):
    seq_count, local_len, width = tokens.shape
    tp_count = lax.axis_size("tp")
    own_seqs = seq_count // tp_count
    first_seq = lax.axis_index("tp") * own_seqs
    own_tokens = lax.dynamic_slice_in_dim(tokens, first_seq, own_seqs, 0)
    own_cotangent = lax.dynamic_slice_in_dim(cotangent, first_seq, own_seqs, 0)
    rows = own_seqs * local_len
    x_own = own_tokens.reshape(rows, width)
    shard_rows = qkv_weight.shape[0]
    head_width = qkv_weight.shape[2]
    ff_width = up_weight.shape[1]
    pad = 128 - norm_gains.shape[1] - row_biases.shape[1]

    first_shard = jnp.concatenate(
        [
            qkv_weight.reshape(shard_rows, 3 * head_width),
            norm_gains,
            row_biases,
            jnp.zeros((shard_rows, pad), B),
        ],
        axis=1,
    )
    first_all = lax.all_gather(first_shard, WEIGHT_AXES, axis=0, tiled=True)
    first_all = first_all.reshape(tp_count, width, first_shard.shape[1])
    x_pieces = [ring_gather(own_tokens[s]) for s in range(own_seqs)]
    second_shard = jnp.concatenate([out_weight, up_weight, down_weight], axis=1)
    second_all = lax.all_gather(second_shard, WEIGHT_AXES, axis=0, tiled=True)
    second_all = second_all.reshape(tp_count, width, second_shard.shape[1])
    w_q = first_all[:, :, :head_width]
    w_kv = first_all[:, :, head_width : 3 * head_width]
    rows_all = jnp.transpose(first_all[0, :, 3 * head_width :]).astype(F)
    gain1, gain2 = rows_all[0], rows_all[1]
    out_bias, shift1, down_bias, shift2 = (rows_all[2 + i] for i in range(4))
    w_out = second_all[:, :, :head_width]
    bias_all = tp_gather(jnp.concatenate([qv_bias.reshape(-1), up_bias]))
    q_bias = bias_all[:, :head_width].astype(F)
    v_bias = bias_all[:, head_width : 2 * head_width].astype(F)
    u_bias = bias_all[:, 2 * head_width :].astype(F)
    kv_bias = jnp.concatenate([jnp.zeros_like(v_bias), v_bias], axis=1)

    def project(block):
        got = (dot(w_kv, block, 1, 1) + kv_bias[:, :, None]).astype(B)
        return got.reshape(tp_count, 2, head_width, block.shape[0])

    x_chunks = [
        [own_tokens[s]] + [jnp.concatenate(pair, axis=0) for pair in x_pieces[s]]
        for s in range(own_seqs)
    ]
    chunk_count = len(x_chunks[0])
    near = (chunk_count + 1) // 2
    q_t, kv_t, om_t, lse, mixed_s = [], [], [], [], []
    for s in range(own_seqs):
        q_s = (dot(w_q, own_tokens[s], 1, 1) + q_bias[:, :, None]).astype(B)
        kv_s = [project(block) for block in x_chunks[s][:near]]
        if near < chunk_count:
            state = attention_forward(q_s, kv_s, None, False, 2048)
            kv_far = [project(block) for block in x_chunks[s][near:]]
            done = attention_forward(q_s, kv_far, state, True, 2048)
            kv_s = kv_s + kv_far
        else:
            done = attention_forward(q_s, kv_s, None, True, 2048)
        q_t.append(q_s)
        kv_t.append(kv_s)
        om_t.append(done[0])
        lse.append(done[1])
        mixed_s.append(done[2])
    mixed_t = jnp.concatenate(mixed_s, axis=2) if own_seqs > 1 else mixed_s[0]
    attn_part = sum(dot(mixed_t[t], w_out[t], 0, 1) for t in range(tp_count))
    x_float = x_own.astype(F)
    first_out, first_norm, first_scale = norm_forward(
        x_float + attn_part + out_bias, gain1, shift1
    )
    first_low = first_out.astype(B)

    act_low, slope, ffn_out = ffn_forward(
        first_low, second_all, u_bias.reshape(1, -1), head_width, ff_width
    )
    ffn_out = ffn_out + down_bias
    grad_final = own_cotangent.reshape(rows, width).astype(F)
    final_out, final_norm, final_scale = norm_forward(first_out + ffn_out, gain2, shift2)
    output = tp_exchange(final_out.astype(B).reshape(own_seqs, local_len, width))
    gain2_grad = jnp.sum(grad_final * final_norm, axis=0)
    shift2_grad = jnp.sum(grad_final, axis=0)
    grad_second = norm_backward(grad_final, final_norm, final_scale, gain2)
    df = grad_second.astype(B)
    down_bias_grad = jnp.sum(df.astype(F), axis=0)
    inner_low, up_bias_grad, back = ffn_backward(df, second_all, slope, head_width, ff_width)
    first_grad = grad_second + back
    gain1_grad = jnp.sum(first_grad * first_norm, axis=0)
    shift1_grad = jnp.sum(first_grad, axis=0)
    resid_grad = norm_backward(first_grad, first_norm, first_scale, gain1)
    da = resid_grad.astype(B)
    out_bias_grad = jnp.sum(da.astype(F), axis=0)
    second_grad = weight_grads(da, first_low, df, mixed_t, inner_low, act_low)
    do_t = dot(w_out, da, 1, 1).astype(B)
    do_t, second_grad = lax.optimization_barrier((do_t, second_grad))
    second_grad = lax.psum_scatter(
        second_grad.reshape(tp_count * width, second_shard.shape[1]),
        WEIGHT_AXES,
        scatter_dimension=0,
        tiled=True,
    ).astype(F)

    v_bias_grad = jnp.sum(do_t.astype(F), axis=2)
    early = sum_all(
        jnp.concatenate(
            [gain1_grad, gain2_grad, out_bias_grad, shift1_grad, down_bias_grad, shift2_grad]
            + [up_bias_grad.reshape(-1), v_bias_grad.reshape(-1)]
        )
    )
    kv_grad = [0.0] * tp_count
    q_grad = [0.0] * tp_count
    q_bias_grad = 0.0
    own_grads = []
    half = local_len // 2
    for s in range(own_seqs):
        do_s = do_t[:, :, s * local_len : (s + 1) * local_len]
        dq = None
        grads = []
        got = None
        for c in reversed(range(chunk_count)):
            dq, dkv = attention_backward(
                q_t[s], kv_t[s][c], do_s, lse[s], om_t[s], dq, c == 0, 1024, 512
            )
            dkv = dkv.reshape(tp_count, 2 * head_width, dkv.shape[3])
            part = sum(dot(dkv[t], w_kv[t], 0, 1) for t in range(tp_count))
            grads.append((c, dkv))
            if c:
                one, two = part[:half], part[half:]
                if got is not None:
                    one = one + got[0].astype(F)
                    two = two + got[1].astype(F)
                one, two, dq = lax.optimization_barrier((one.astype(B), two.astype(B), dq))
                got = ring_return(one, two)
        dq_low = dq
        for c, dkv in grads:
            kv_grad = [kv_grad[t] + dot(x_chunks[s][c], dkv[t], 0, 1) for t in range(tp_count)]
        q_bias_grad = q_bias_grad + jnp.sum(dq_low.astype(F), axis=2)
        q_grad = [q_grad[t] + dot(own_tokens[s], dq_low[t], 0, 1) for t in range(tp_count)]
        part = part + sum(dot(dq_low[t], w_q[t], 0, 1) for t in range(tp_count))
        if got is not None:
            part = part + jnp.concatenate(got, axis=0).astype(F)
        own_grads.append(part)
    q_bias_grad = sum_all(q_bias_grad.reshape(-1))
    qkv_grad = jnp.stack(
        [jnp.concatenate([q_grad[t], kv_grad[t]], axis=1).astype(B) for t in range(tp_count)]
    )
    qkv_grad = qkv_grad.reshape(tp_count, width // shard_rows, shard_rows, 3 * head_width)
    cut = (3 * head_width // 256) * 128
    qkv_grad = jnp.concatenate(
        [
            scatter_sum(qkv_grad[..., :cut], ("tp", "fsdp", "ctx")),
            scatter_sum(qkv_grad[..., cut:], ("fsdp", "tp", "ctx")),
        ],
        axis=1,
    )
    tokens_grad = resid_grad.reshape(own_seqs, local_len, width) + jnp.stack(own_grads)
    tokens_out = tp_exchange(tokens_grad.astype(B))

    member = lax.axis_index("fsdp") * lax.axis_size("ctx") + lax.axis_index("ctx")
    own_tp = lax.axis_index("tp")
    six = lax.dynamic_slice_in_dim(
        early[: 6 * width].reshape(6, width), member * shard_rows, shard_rows, 1
    )
    six = jnp.transpose(six)
    up_total = lax.dynamic_slice_in_dim(early, 6 * width + own_tp * ff_width, ff_width, 0)
    v_total = lax.dynamic_slice_in_dim(
        early, 6 * width + tp_count * ff_width + own_tp * head_width, head_width, 0
    )
    q_total = lax.dynamic_slice_in_dim(q_bias_grad, own_tp * head_width, head_width, 0)
    return (
        output,
        tokens_out,
        qkv_grad.reshape(shard_rows, 3, head_width),
        jnp.stack([q_total, v_total]),
        second_grad[:, :head_width],
        second_grad[:, head_width : head_width + ff_width],
        up_total,
        second_grad[:, head_width + ff_width :],
        six[:, :2],
        six[:, 2:],
    )


def solution(mesh):
    in_specs = (
        P("fsdp", "ctx", None),
        P(("fsdp", "ctx"), None, "tp"),
        P(None, "tp"),
        P(("fsdp", "ctx"), "tp"),
        P(("fsdp", "ctx"), "tp"),
        P("tp"),
        P(("fsdp", "ctx"), "tp"),
        P(("fsdp", "ctx"), None),
        P(("fsdp", "ctx"), None),
        P("fsdp", "ctx", None),
    )
    out_specs = (
        P("fsdp", ("ctx", "tp"), None),
        P("fsdp", ("ctx", "tp"), None),
        P(("fsdp", "ctx"), None, "tp"),
        P(None, "tp"),
        P(("fsdp", "ctx"), "tp"),
        P(("fsdp", "ctx"), "tp"),
        P("tp"),
        P(("fsdp", "ctx"), "tp"),
        P(("fsdp", "ctx"), None),
        P(("fsdp", "ctx"), None),
    )
    return jax.shard_map(layer, mesh=mesh, in_specs=in_specs, out_specs=out_specs, check_vma=False)
```

```python
import jax
import jax.numpy as jnp
from jax import lax
from jax.experimental import pallas as pl
from jax.experimental.pallas import tpu as pltpu
from jax.sharding import PartitionSpec as P


HD = 64
B = jnp.bfloat16
F = jnp.float32
epsilon = 1e-12
score_scale = 0.125
LOG2E = 1.4426950408889634
WEIGHT_AXES = ("tp", "fsdp", "ctx")


def dot(left, right, left_dim, right_dim):
    return lax.dot_general(
        left, right, (((left_dim,), (right_dim,)), ((), ())), preferred_element_type=F
    )


def split_low(value, count):
    parts = []
    for _ in range(count):
        part = value.astype(B)
        parts.append(part)
        value = value - part.astype(F)
    return parts


def pick_block(size, wanted):
    while size % wanted:
        wanted //= 2
    return wanted


def forward_kernel(*refs, chunks, first, last, bk):
    q_ref = refs[0]
    kv_refs = refs[1 : 1 + chunks]
    at = 1 + chunks
    if not first:
        o_in, stat_in = refs[at : at + 2]
        at += 2
    o_ref, stat_ref = refs[at : at + 2]
    qx, kx, vx = refs[-3:]
    rows = q_ref.shape[-1]
    keys = kx.shape[-1]
    scaled = q_ref[0].astype(F) * (score_scale * LOG2E)
    high, rest = split_low(scaled, 2)
    qx[0:HD, :] = high
    qx[HD : 2 * HD, :] = rest
    size = keys // chunks
    for c, kv_ref in enumerate(kv_refs):
        at = c * size
        kx[0:HD, at : at + size] = kv_ref[0, 0]
        kx[HD : 2 * HD, at : at + size] = kv_ref[0, 0]
        vx[0:HD, at : at + size] = kv_ref[0, 1]
    vx[HD : HD + 16, :] = jnp.ones((16, keys), B)

    def step(i, carry):
        row_max, mixed, total = carry
        off = pl.multiple_of(i * bk, bk)
        scores = dot(kx[:, pl.ds(off, bk)], qx[...], 0, 0)
        new_max = jnp.maximum(row_max, jnp.max(scores, axis=0, keepdims=True))
        probs = jnp.exp2(scores - new_max).astype(B)
        scale = jnp.exp2(row_max - new_max)
        more = dot(vx[:, pl.ds(off, bk)], probs, 1, 0)
        return new_max, mixed * scale + more[0:HD, :], total * scale + more[HD : HD + 1, :]

    if first:
        start = (
            jnp.full((1, rows), -jnp.inf, F),
            jnp.zeros((HD, rows), F),
            jnp.zeros((1, rows), F),
        )
    else:
        start = (stat_in[0, 0, 0:1, :], o_in[0], stat_in[0, 0, 1:2, :])
    row_max, mixed, total = lax.fori_loop(0, keys // bk, step, start)
    if last:
        mixed = mixed / total
        o_ref[0] = mixed
        refs[-4][0] = mixed.astype(B)
        stat_ref[0, 0] = row_max + jnp.log2(total)
    else:
        o_ref[0] = mixed
        stat_ref[0, 0, 0:1, :] = row_max
        stat_ref[0, 0, 1:2, :] = total


def attention_forward(q_t, kv_list, state, last, bk):
    parts, width, rows = q_t.shape
    chunks = len(kv_list)
    keys = kv_list[0].shape[3]
    heads = width // HD
    bk = pick_block(keys * chunks, bk)
    first = state is None
    row_spec = pl.BlockSpec((1, HD, rows), lambda t, h: (t, h, 0))
    two_spec = pl.BlockSpec((1, 1, 2, rows), lambda t, h: (t, h, 0, 0))
    one_spec = pl.BlockSpec((1, 1, 1, rows), lambda t, h: (t, h, 0, 0))
    key_spec = pl.BlockSpec((1, 2, HD, keys), lambda t, h: (t, 0, h, 0))
    total = parts * heads * rows * keys * chunks
    return pl.pallas_call(
        lambda *refs: forward_kernel(*refs, chunks=chunks, first=first, last=last, bk=bk),
        grid=(parts, heads),
        in_specs=[row_spec] + [key_spec] * chunks + ([] if first else [row_spec, two_spec]),
        out_specs=[row_spec, one_spec, row_spec] if last else [row_spec, two_spec],
        out_shape=[
            jax.ShapeDtypeStruct((parts, width, rows), F),
            jax.ShapeDtypeStruct((parts, heads, 1 if last else 2, rows), F),
        ]
        + ([jax.ShapeDtypeStruct((parts, width, rows), B)] if last else []),
        scratch_shapes=[
            pltpu.VMEM((2 * HD, rows), B),
            pltpu.VMEM((2 * HD, keys * chunks), B),
            pltpu.VMEM((HD + 16, keys * chunks), B),
        ],
        compiler_params=pltpu.CompilerParams(
            vmem_limit_bytes=56 << 20, dimension_semantics=("arbitrary", "arbitrary")
        ),
        cost_estimate=pl.CostEstimate(
            flops=1024 * total, transcendentals=total, bytes_accessed=16 << 20
        ),
        name="attn_forward",
    )(q_t, *kv_list, *(() if first else state))


def backward_kernel(*refs, first, bk, bq):
    q_ref, kv_ref, do_ref, lse_ref, om_ref = refs[:5]
    dq_ref, dkv_ref, qx, kx, dx, vx, dq_acc = refs[-7:]
    rows = q_ref.shape[-1]
    keys = kv_ref.shape[-1]
    scaled = q_ref[0].astype(F) * (score_scale * LOG2E)
    high, rest = split_low(scaled, 2)
    sub = lax.broadcasted_iota(jnp.int32, (16, rows), 0)

    def stacked(value):
        block = jnp.zeros((16, rows), F)
        for j, part in enumerate(split_low(value, 3)):
            block = jnp.where(sub == j, jnp.broadcast_to(part.astype(F), (16, rows)), block)
        return block.astype(B)

    qx[0:HD, :] = high
    qx[HD : 2 * HD, :] = rest
    qx[2 * HD : 2 * HD + 16, :] = stacked(lse_ref[0, 0])
    dx[0:HD, :] = do_ref[0]
    delta = jnp.sum(om_ref[0] * do_ref[0].astype(F), axis=0, keepdims=True)
    dx[HD : HD + 16, :] = stacked(delta)
    kx[0:HD, :] = kv_ref[0, 0]
    kx[HD : 2 * HD, :] = kv_ref[0, 0]
    kx[2 * HD : 2 * HD + 16, :] = jnp.full((16, keys), -1.0, B)
    vx[0:HD, :] = kv_ref[0, 1]
    vx[HD : HD + 16, :] = jnp.full((16, keys), -1.0, B)
    dq_acc[...] = jnp.zeros_like(dq_acc)

    def step(i, carry):
        off = pl.multiple_of(i * bk, bk)
        k_part = kx[:, pl.ds(off, bk)]
        v_part = vx[:, pl.ds(off, bk)]
        dk_part = jnp.zeros((HD, bk), F)
        dv_part = jnp.zeros((HD, bk), F)
        for j in range(0, rows, bq):
            probs = jnp.exp2(dot(qx[:, j : j + bq], k_part, 0, 0))
            prob_grad = dot(dx[:, j : j + bq], v_part, 0, 0)
            score_low = (probs * prob_grad).astype(B)
            prob_low = probs.astype(B)
            dv_part = dv_part + dot(dx[0:HD, j : j + bq], prob_low, 1, 0)
            dk_part = dk_part + dot(q_ref[0, :, j : j + bq], score_low, 1, 0)
            dq_acc[j : j + bq, :] += dot(score_low, k_part[0:HD, :], 1, 1)
        dkv_ref[0, 0, :, pl.ds(off, bk)] = (dk_part * score_scale).astype(B)
        dkv_ref[0, 1, :, pl.ds(off, bk)] = dv_part.astype(B)
        return carry

    lax.fori_loop(0, keys // bk, step, 0)
    total = jnp.transpose(dq_acc[...] * score_scale)
    if not first:
        total = total + refs[5][0]
    dq_ref[0] = total.astype(dq_ref.dtype)


def attention_backward(q_t, kv_t, do_t, lse, om_t, dq_t, last, bk, bq):
    parts, width, rows = q_t.shape
    keys = kv_t.shape[3]
    heads = width // HD
    bk = pick_block(keys, bk)
    bq = pick_block(rows, bq)
    first = dq_t is None
    total = parts * heads * rows * keys
    row_spec = pl.BlockSpec((1, HD, rows), lambda t, h: (t, h, 0))
    stat_spec = pl.BlockSpec((1, 1, 1, rows), lambda t, h: (t, h, 0, 0))
    key_spec = pl.BlockSpec((1, 2, HD, keys), lambda t, h: (t, 0, h, 0))
    return pl.pallas_call(
        lambda *refs: backward_kernel(*refs, first=first, bk=bk, bq=bq),
        grid=(parts, heads),
        in_specs=[row_spec, key_spec, row_spec, stat_spec, row_spec]
        + ([] if first else [row_spec]),
        out_specs=[row_spec, key_spec],
        out_shape=[
            jax.ShapeDtypeStruct((parts, width, rows), B if last else F),
            jax.ShapeDtypeStruct((parts, 2, width, keys), B),
        ],
        scratch_shapes=[
            pltpu.VMEM((2 * HD + 16, rows), B),
            pltpu.VMEM((2 * HD + 16, keys), B),
            pltpu.VMEM((HD + 16, rows), B),
            pltpu.VMEM((HD + 16, keys), B),
            pltpu.VMEM((rows, HD), F),
        ],
        compiler_params=pltpu.CompilerParams(
            vmem_limit_bytes=56 << 20, dimension_semantics=("arbitrary", "arbitrary")
        ),
        cost_estimate=pl.CostEstimate(
            flops=2048 * total, transcendentals=total, bytes_accessed=16 << 20
        ),
        name="attn_backward",
    )(q_t, kv_t, do_t, lse, om_t, *([] if first else [dq_t]))


def gelu_both(u):
    z = jnp.abs(u) * 0.7071067811865476
    t = 1.0 / (1.0 + 0.5 * z)
    series = 0.17087277
    for c in (
        -0.82215223,
        1.48851587,
        -1.13520398,
        0.27886807,
        -0.18628806,
        0.09678418,
        0.37409196,
        1.00002368,
        -1.26551223,
    ):
        series = series * t + c
    bell = jnp.exp(u * u * -0.5)
    tail = (0.5 * t) * bell * jnp.exp(series)
    below = jnp.where(u >= 0, 1.0 - tail, tail)
    return u * below, below + u * (bell * 0.3989422804014327)


def ffn_forward_kernel(y_ref, up_ref, down_ref, bias_ref, act_ref, slope_ref, out_ref, *, br):
    start = (pl.program_id(0) == 0) & (pl.program_id(1) == 0)

    @pl.when(start)
    def _():
        out_ref[...] = jnp.zeros_like(out_ref)

    for r in range(0, y_ref.shape[0], br):
        u = dot(y_ref[r : r + br, :], up_ref[0], 1, 0) + bias_ref[...]
        act, slope = gelu_both(u)
        low = act.astype(B)
        act_ref[r : r + br, :] = low
        slope_ref[r : r + br, :] = slope
        out_ref[r : r + br, :] += dot(low, down_ref[0], 1, 1)


def ffn_backward_kernel(df_ref, up_ref, down_ref, slope_ref, du_ref, sum_ref, out_ref, *, br):
    start = (pl.program_id(0) == 0) & (pl.program_id(1) == 0)

    @pl.when(start)
    def _():
        out_ref[...] = jnp.zeros_like(out_ref)

    total = jnp.zeros(sum_ref.shape, F)
    for r in range(0, df_ref.shape[0], br):
        du = (dot(df_ref[r : r + br, :], down_ref[0], 1, 0) * slope_ref[r : r + br, :]).astype(B)
        du_ref[r : r + br, :] = du
        total = total + jnp.sum(du.astype(F), axis=0, keepdims=True)
        out_ref[r : r + br, :] += dot(du, up_ref[0], 1, 1)
    sum_ref[...] = total


def ffn_specs(rows, width, weights, block, ff_width):
    per = ff_width // block
    up_spec = pl.BlockSpec((1, width, block), lambda t, j: (t, 0, j))
    down_spec = pl.BlockSpec((1, width, block), lambda t, j: (t, 0, per + j))
    row_spec = pl.BlockSpec((rows, width), lambda t, j: (0, 0))
    hidden_spec = pl.BlockSpec((rows, block), lambda t, j: (0, t * per + j))
    vector_spec = pl.BlockSpec((1, block), lambda t, j: (0, t * per + j))
    return (weights.shape[0], per), up_spec, down_spec, row_spec, hidden_spec, vector_spec


FFN_PARAMS = pltpu.CompilerParams(
    vmem_limit_bytes=56 << 20, dimension_semantics=("arbitrary", "arbitrary")
)


def ffn_forward(y_low, weights, bias, block, ff_width):
    rows, width = y_low.shape
    grid, up_spec, down_spec, row_spec, hidden_spec, vector_spec = ffn_specs(
        rows, width, weights, block, ff_width
    )
    hidden = grid[0] * ff_width
    return pl.pallas_call(
        lambda *refs: ffn_forward_kernel(*refs, br=pick_block(rows, 256)),
        grid=grid,
        in_specs=[row_spec, up_spec, down_spec, vector_spec],
        out_specs=[hidden_spec, hidden_spec, row_spec],
        out_shape=[
            jax.ShapeDtypeStruct((rows, hidden), B),
            jax.ShapeDtypeStruct((rows, hidden), F),
            jax.ShapeDtypeStruct((rows, width), F),
        ],
        compiler_params=FFN_PARAMS,
        name="ffn_forward",
    )(y_low, weights, weights, bias)


def ffn_backward(df, weights, slope, block, ff_width):
    rows, width = df.shape
    grid, up_spec, down_spec, row_spec, hidden_spec, vector_spec = ffn_specs(
        rows, width, weights, block, ff_width
    )
    hidden = grid[0] * ff_width
    return pl.pallas_call(
        lambda *refs: ffn_backward_kernel(*refs, br=pick_block(rows, 256)),
        grid=grid,
        in_specs=[row_spec, up_spec, down_spec, hidden_spec],
        out_specs=[hidden_spec, vector_spec, row_spec],
        out_shape=[
            jax.ShapeDtypeStruct((rows, hidden), B),
            jax.ShapeDtypeStruct((1, hidden), F),
            jax.ShapeDtypeStruct((rows, width), F),
        ],
        compiler_params=FFN_PARAMS,
        name="ffn_backward",
    )(df, weights, weights, slope)


def weight_grad_kernel(da_ref, y_ref, df_ref, mixed_ref, du_ref, act_ref, out_ref, *, per):
    j = pl.program_id(1)

    @pl.when(j == 2 * per)
    def _():
        out_ref[0, :, : mixed_ref.shape[1]] = dot(da_ref[...], mixed_ref[0], 0, 1).astype(B)

    @pl.when(j < per)
    def _():
        out_ref[0] = dot(y_ref[...], du_ref[...], 0, 0).astype(B)

    @pl.when((j >= per) & (j < 2 * per))
    def _():
        out_ref[0] = dot(df_ref[...], act_ref[...], 0, 0).astype(B)


def weight_grads(da, y_low, df, mixed_t, du, act, block):
    rows, width = da.shape
    parts, head_width, _ = mixed_t.shape
    per = du.shape[1] // parts // block
    row_spec = pl.BlockSpec((rows, width), lambda t, j: (0, 0))
    return pl.pallas_call(
        lambda *refs: weight_grad_kernel(*refs, per=per),
        grid=(parts, 1 + 2 * per),
        in_specs=[
            row_spec,
            row_spec,
            row_spec,
            pl.BlockSpec((1, head_width, rows), lambda t, j: (t, 0, 0)),
            pl.BlockSpec((rows, block), lambda t, j: (0, t * per + jnp.clip(j, 0, per - 1))),
            pl.BlockSpec((rows, block), lambda t, j: (0, t * per + jnp.clip(j - per, 0, per - 1))),
        ],
        out_specs=pl.BlockSpec((1, width, block), lambda t, j: (t, 0, j)),
        out_shape=jax.ShapeDtypeStruct((parts, width, head_width + 2 * per * block), B),
        compiler_params=FFN_PARAMS,
        name="weight_grads",
    )(da, y_low, df, mixed_t, du, act)


def ring_gather(block):
    count = lax.axis_size("ctx")
    up = [(i, (i + 1) % count) for i in range(count)]
    down = [((i + 1) % count, i) for i in range(count)]
    half = block.shape[0] // 2
    first, second = block[:half], block[half:]
    pieces = []
    for _ in range(1, count):
        first = lax.ppermute(first, "ctx", up)
        second = lax.ppermute(second, "ctx", down)
        pieces.append((first, second))
    return pieces


def ring_return(first, second):
    count = lax.axis_size("ctx")
    up = [(i, (i + 1) % count) for i in range(count)]
    down = [((i + 1) % count, i) for i in range(count)]
    return lax.ppermute(first, "ctx", down), lax.ppermute(second, "ctx", up)


def scatter_sum(blocks, order):
    sizes = {axis: lax.axis_size(axis) for axis in WEIGHT_AXES}
    bits = []
    for axis in WEIGHT_AXES:
        bit = sizes[axis] // 2
        while bit:
            bits.append((axis, bit))
            bit //= 2
    left = blocks.reshape((2,) * len(bits) + blocks.shape[2:])
    todo = sorted(
        bits,
        key=lambda one: (one != ("fsdp", 1), order.index(one[0]), -one[1]),
    )
    for axis, bit in todo:
        dim = bits.index((axis, bit))
        bits.remove((axis, bit))
        mine = (lax.axis_index(axis) // bit) % 2
        sent = lax.dynamic_index_in_dim(left, 1 - mine, dim, keepdims=False)
        kept = lax.dynamic_index_in_dim(left, mine, dim, keepdims=False)
        got = lax.ppermute(sent, axis, [(i, i ^ bit) for i in range(sizes[axis])])
        total = kept.astype(F) + got.astype(F)
        left = total.astype(B) if bits else total
    return left


def sum_all(vector):
    every = lax.all_gather(vector.reshape(-1, 128), ("fsdp", "ctx", "tp"), axis=0)
    return jnp.sum(every, axis=0).reshape(-1)


def sum_steps(vector):
    for axis in ("fsdp", "tp", "ctx"):
        size = lax.axis_size(axis)
        bit = 1
        while bit < size:
            vector = vector + lax.ppermute(vector, axis, [(i, i ^ bit) for i in range(size)])
            bit *= 2
    return vector


def tp_gather(vector):
    size = lax.axis_size("tp")
    own = lax.axis_index("tp")
    out = jnp.zeros((size,) + vector.shape, vector.dtype)
    out = lax.dynamic_update_index_in_dim(out, vector, own, 0)
    for shift in range(1, size):
        got = lax.ppermute(vector, "tp", [(i, (i + shift) % size) for i in range(size)])
        out = lax.dynamic_update_index_in_dim(out, got, (own - shift) % size, 0)
    return out


def tp_exchange(rows):
    size = lax.axis_size("tp")
    own = lax.axis_index("tp")
    seqs, length, width = rows.shape
    split = rows.reshape(seqs, size, length // size, width)
    out = jnp.zeros((size, seqs, length // size, width), rows.dtype)
    kept = lax.dynamic_index_in_dim(split, own, 1, keepdims=False)
    out = lax.dynamic_update_index_in_dim(out, kept, own, 0)
    for shift in range(1, size):
        sent = lax.dynamic_index_in_dim(split, (own + shift) % size, 1, keepdims=False)
        got = lax.ppermute(sent, "tp", [(i, (i + shift) % size) for i in range(size)])
        out = lax.dynamic_update_index_in_dim(out, got, (own - shift) % size, 0)
    return out.reshape(size * seqs, length // size, width)


def norm_forward(hidden, gain, shift):
    center = hidden - jnp.mean(hidden, axis=-1, keepdims=True)
    inv_scale = lax.rsqrt(jnp.mean(center * center, axis=-1, keepdims=True) + epsilon)
    normed = center * inv_scale
    return (normed * gain + shift, normed, inv_scale)


def norm_backward(grad_out, normed, inv_scale, gain):
    grad_norm = grad_out * gain
    return inv_scale * (
        grad_norm
        - jnp.mean(grad_norm, axis=-1, keepdims=True)
        - normed * jnp.mean(grad_norm * normed, axis=-1, keepdims=True)
    )


def layer(
    tokens,
    qkv_weight,
    qv_bias,
    out_weight,
    up_weight,
    up_bias,
    down_weight,
    norm_gains,
    row_biases,
    cotangent,
):
    seq_count, local_len, width = tokens.shape
    tp_count = lax.axis_size("tp")
    own_seqs = seq_count // tp_count
    first_seq = lax.axis_index("tp") * own_seqs
    own_tokens = lax.dynamic_slice_in_dim(tokens, first_seq, own_seqs, 0)
    own_cotangent = lax.dynamic_slice_in_dim(cotangent, first_seq, own_seqs, 0)
    rows = own_seqs * local_len
    x_own = own_tokens.reshape(rows, width)
    shard_rows = qkv_weight.shape[0]
    head_width = qkv_weight.shape[2]
    ff_width = up_weight.shape[1]
    pad = 128 - norm_gains.shape[1] - row_biases.shape[1]

    first_shard = jnp.concatenate(
        [
            qkv_weight.reshape(shard_rows, 3 * head_width),
            norm_gains,
            row_biases,
            jnp.zeros((shard_rows, pad), B),
        ],
        axis=1,
    )
    first_all = lax.all_gather(first_shard, WEIGHT_AXES, axis=0, tiled=True)
    first_all = first_all.reshape(tp_count, width, first_shard.shape[1])
    x_pieces = [ring_gather(own_tokens[s]) for s in range(own_seqs)]
    second_shard = jnp.concatenate([up_weight, down_weight, out_weight], axis=1)
    second_all = lax.all_gather(second_shard, WEIGHT_AXES, axis=0, tiled=True)
    second_all = second_all.reshape(tp_count, width, second_shard.shape[1])
    w_q = first_all[:, :, :head_width]
    w_kv = first_all[:, :, head_width : 3 * head_width]
    rows_all = jnp.transpose(first_all[0, :, 3 * head_width :]).astype(F)
    gain1, gain2 = rows_all[0], rows_all[1]
    out_bias, shift1, down_bias, shift2 = (rows_all[2 + i] for i in range(4))
    w_out = second_all[:, :, 2 * ff_width :]
    bias_all = tp_gather(jnp.concatenate([qv_bias.reshape(-1), up_bias]))
    q_bias = bias_all[:, :head_width].astype(F)
    v_bias = bias_all[:, head_width : 2 * head_width].astype(F)
    u_bias = bias_all[:, 2 * head_width :].astype(F)
    kv_bias = jnp.concatenate([jnp.zeros_like(v_bias), v_bias], axis=1)

    def project(block):
        got = (dot(w_kv, block, 1, 1) + kv_bias[:, :, None]).astype(B)
        return got.reshape(tp_count, 2, head_width, block.shape[0])

    x_chunks = [
        [own_tokens[s]] + [jnp.concatenate(pair, axis=0) for pair in x_pieces[s]]
        for s in range(own_seqs)
    ]
    chunk_count = len(x_chunks[0])
    near = (chunk_count + 1) // 2
    q_t, kv_t, om_t, lse, mixed_s = [], [], [], [], []
    for s in range(own_seqs):
        q_s = (dot(w_q, own_tokens[s], 1, 1) + q_bias[:, :, None]).astype(B)
        kv_s = [project(x_chunks[s][0])]
        kv_s = kv_s + [project(block) for block in x_chunks[s][1:near]]
        if near < chunk_count:
            state = attention_forward(q_s, kv_s, None, False, 2048)
            kv_far = [project(block) for block in x_chunks[s][near:]]
            done = attention_forward(q_s, kv_far, state, True, 2048)
            kv_s = kv_s + kv_far
        else:
            done = attention_forward(q_s, kv_s, None, True, 2048)
        q_t.append(q_s)
        kv_t.append(kv_s)
        om_t.append(done[0])
        lse.append(done[1])
        mixed_s.append(done[2])
    mixed_t = jnp.concatenate(mixed_s, axis=2) if own_seqs > 1 else mixed_s[0]
    attn_part = sum(dot(mixed_t[t], w_out[t], 0, 1) for t in range(tp_count))
    x_float = x_own.astype(F)
    first_out, first_norm, first_scale = norm_forward(
        x_float + attn_part + out_bias, gain1, shift1
    )
    first_low = first_out.astype(B)

    block = ff_width // 2
    act_low, slope, ffn_out = ffn_forward(
        first_low, second_all, u_bias.reshape(1, -1), block, ff_width
    )
    ffn_out = ffn_out + down_bias
    grad_final = own_cotangent.reshape(rows, width).astype(F)
    final_out, final_norm, final_scale = norm_forward(first_out + ffn_out, gain2, shift2)
    output = tp_exchange(final_out.astype(B).reshape(own_seqs, local_len, width))
    gain2_grad = jnp.sum(grad_final * final_norm, axis=0)
    shift2_grad = jnp.sum(grad_final, axis=0)
    grad_second = norm_backward(grad_final, final_norm, final_scale, gain2)
    df = grad_second.astype(B)
    down_bias_grad = jnp.sum(df.astype(F), axis=0)
    inner_low, up_bias_grad, back = ffn_backward(df, second_all, slope, block, ff_width)
    first_grad = grad_second + back
    gain1_grad = jnp.sum(first_grad * first_norm, axis=0)
    shift1_grad = jnp.sum(first_grad, axis=0)
    resid_grad = norm_backward(first_grad, first_norm, first_scale, gain1)
    da = resid_grad.astype(B)
    out_bias_grad = jnp.sum(da.astype(F), axis=0)
    second_grad = weight_grads(da, first_low, df, mixed_t, inner_low, act_low, block)
    do_t = dot(w_out, da, 1, 1).astype(B)
    do_t, second_grad = lax.optimization_barrier((do_t, second_grad))
    second_grad = lax.psum_scatter(
        second_grad.reshape(tp_count * width, second_shard.shape[1]),
        WEIGHT_AXES,
        scatter_dimension=0,
        tiled=True,
    ).astype(F)

    v_bias_grad = jnp.sum(do_t.astype(F), axis=2)
    early = sum_all(
        jnp.concatenate(
            [gain1_grad, gain2_grad, out_bias_grad, shift1_grad, down_bias_grad, shift2_grad]
            + [up_bias_grad.reshape(-1), v_bias_grad.reshape(-1)]
        )
    )
    kv_grad = [0.0] * tp_count
    q_grad = [0.0] * tp_count
    q_bias_grad = 0.0
    own_grads = []
    half = local_len // 2
    for s in range(own_seqs):
        do_s = do_t[:, :, s * local_len : (s + 1) * local_len]
        dq = None
        grads = []
        got = None
        for c in reversed(range(chunk_count)):
            dq, dkv = attention_backward(
                q_t[s], kv_t[s][c], do_s, lse[s], om_t[s], dq, c == 0, 1024, 512
            )
            dkv = dkv.reshape(tp_count, 2 * head_width, dkv.shape[3])
            part = sum(dot(dkv[t], w_kv[t], 0, 1) for t in range(tp_count))
            grads.append((c, dkv))
            if c:
                one, two = part[:half], part[half:]
                if got is not None:
                    one = one + got[0].astype(F)
                    two = two + got[1].astype(F)
                one, two, dq = lax.optimization_barrier((one.astype(B), two.astype(B), dq))
                got = ring_return(one, two)
        dq_low = dq
        for c, dkv in grads:
            kv_grad = [kv_grad[t] + dot(x_chunks[s][c], dkv[t], 0, 1) for t in range(tp_count)]
        q_bias_grad = q_bias_grad + jnp.sum(dq_low.astype(F), axis=2)
        q_grad = [q_grad[t] + dot(own_tokens[s], dq_low[t], 0, 1) for t in range(tp_count)]
        part = part + sum(dot(dq_low[t], w_q[t], 0, 1) for t in range(tp_count))
        if got is not None:
            part = part + jnp.concatenate(got, axis=0).astype(F)
        own_grads.append(part)
    q_bias_grad = sum_steps(q_bias_grad.reshape(-1))
    qkv_grad = jnp.stack(
        [jnp.concatenate([q_grad[t], kv_grad[t]], axis=1).astype(B) for t in range(tp_count)]
    )
    qkv_grad = qkv_grad.reshape(tp_count, width // shard_rows, shard_rows, 3 * head_width)
    cut = (3 * head_width // 256) * 128
    qkv_grad = jnp.concatenate(
        [
            scatter_sum(qkv_grad[..., :cut], ("tp", "fsdp", "ctx")),
            scatter_sum(qkv_grad[..., cut:], ("fsdp", "tp", "ctx")),
        ],
        axis=1,
    )
    tokens_grad = resid_grad.reshape(own_seqs, local_len, width) + jnp.stack(own_grads)
    tokens_out = tp_exchange(tokens_grad.astype(B))

    member = lax.axis_index("fsdp") * lax.axis_size("ctx") + lax.axis_index("ctx")
    own_tp = lax.axis_index("tp")
    six = lax.dynamic_slice_in_dim(
        early[: 6 * width].reshape(6, width), member * shard_rows, shard_rows, 1
    )
    six = jnp.transpose(six)
    up_total = lax.dynamic_slice_in_dim(early, 6 * width + own_tp * ff_width, ff_width, 0)
    v_total = lax.dynamic_slice_in_dim(
        early, 6 * width + tp_count * ff_width + own_tp * head_width, head_width, 0
    )
    q_total = lax.dynamic_slice_in_dim(q_bias_grad, own_tp * head_width, head_width, 0)
    return (
        output,
        tokens_out,
        qkv_grad.reshape(shard_rows, 3, head_width),
        jnp.stack([q_total, v_total]),
        second_grad[:, 2 * ff_width :],
        second_grad[:, :ff_width],
        up_total,
        second_grad[:, ff_width : 2 * ff_width],
        six[:, :2],
        six[:, 2:],
    )


def solution(mesh):
    in_specs = (
        P("fsdp", "ctx", None),
        P(("fsdp", "ctx"), None, "tp"),
        P(None, "tp"),
        P(("fsdp", "ctx"), "tp"),
        P(("fsdp", "ctx"), "tp"),
        P("tp"),
        P(("fsdp", "ctx"), "tp"),
        P(("fsdp", "ctx"), None),
        P(("fsdp", "ctx"), None),
        P("fsdp", "ctx", None),
    )
    out_specs = (
        P("fsdp", ("ctx", "tp"), None),
        P("fsdp", ("ctx", "tp"), None),
        P(("fsdp", "ctx"), None, "tp"),
        P(None, "tp"),
        P(("fsdp", "ctx"), "tp"),
        P(("fsdp", "ctx"), "tp"),
        P("tp"),
        P(("fsdp", "ctx"), "tp"),
        P(("fsdp", "ctx"), None),
        P(("fsdp", "ctx"), None),
    )
    return jax.shard_map(layer, mesh=mesh, in_specs=in_specs, out_specs=out_specs, check_vma=False)
```

```python
import jax
import jax.numpy as jnp
from jax import lax
from jax.experimental import pallas as pl
from jax.experimental.pallas import tpu as pltpu
from jax.sharding import PartitionSpec as P


HD = 64
B = jnp.bfloat16
F = jnp.float32
epsilon = 1e-12
score_scale = 0.125
LOG2E = 1.4426950408889634
WEIGHT_AXES = ("tp", "fsdp", "ctx")


def dot(left, right, left_dim, right_dim):
    return lax.dot_general(
        left, right, (((left_dim,), (right_dim,)), ((), ())), preferred_element_type=F
    )


def split_low(value, count):
    parts = []
    for _ in range(count):
        part = value.astype(B)
        parts.append(part)
        value = value - part.astype(F)
    return parts


def pick_block(size, wanted):
    while size % wanted:
        wanted //= 2
    return wanted


def forward_kernel(*refs, chunks, first, last, bk):
    q_ref = refs[0]
    kv_refs = refs[1 : 1 + chunks]
    at = 1 + chunks
    if not first:
        o_in, stat_in = refs[at : at + 2]
        at += 2
    o_ref, stat_ref = refs[at : at + 2]
    qx, kx, vx = refs[-3:]
    rows = q_ref.shape[-1]
    keys = kx.shape[-1]
    scaled = q_ref[0].astype(F) * (score_scale * LOG2E)
    high, rest = split_low(scaled, 2)
    qx[0:HD, :] = high
    qx[HD : 2 * HD, :] = rest
    size = keys // chunks
    for c, kv_ref in enumerate(kv_refs):
        at = c * size
        kx[0:HD, at : at + size] = kv_ref[0, 0]
        kx[HD : 2 * HD, at : at + size] = kv_ref[0, 0]
        vx[0:HD, at : at + size] = kv_ref[0, 1]
    vx[HD : HD + 16, :] = jnp.ones((16, keys), B)

    def step(i, carry):
        row_max, mixed, total = carry
        off = pl.multiple_of(i * bk, bk)
        scores = dot(kx[:, pl.ds(off, bk)], qx[...], 0, 0)
        new_max = jnp.maximum(row_max, jnp.max(scores, axis=0, keepdims=True))
        probs = jnp.exp2(scores - new_max).astype(B)
        scale = jnp.exp2(row_max - new_max)
        more = dot(vx[:, pl.ds(off, bk)], probs, 1, 0)
        return new_max, mixed * scale + more[0:HD, :], total * scale + more[HD : HD + 1, :]

    if first:
        start = (
            jnp.full((1, rows), -jnp.inf, F),
            jnp.zeros((HD, rows), F),
            jnp.zeros((1, rows), F),
        )
    else:
        start = (stat_in[0, 0, 0:1, :], o_in[0], stat_in[0, 0, 1:2, :])
    row_max, mixed, total = lax.fori_loop(0, keys // bk, step, start)
    if last:
        mixed = mixed * (1.0 / total)
        o_ref[0] = mixed
        refs[-4][0] = mixed.astype(B)
        stat_ref[0, 0] = row_max + jnp.log2(total)
    else:
        o_ref[0] = mixed
        stat_ref[0, 0, 0:1, :] = row_max
        stat_ref[0, 0, 1:2, :] = total


def attention_forward(q_t, kv_list, state, last, bk):
    parts, width, rows = q_t.shape
    chunks = len(kv_list)
    keys = kv_list[0].shape[3]
    heads = width // HD
    bk = pick_block(keys * chunks, bk)
    first = state is None
    row_spec = pl.BlockSpec((1, HD, rows), lambda t, h: (t, h, 0))
    two_spec = pl.BlockSpec((1, 1, 2, rows), lambda t, h: (t, h, 0, 0))
    one_spec = pl.BlockSpec((1, 1, 1, rows), lambda t, h: (t, h, 0, 0))
    key_spec = pl.BlockSpec((1, 2, HD, keys), lambda t, h: (t, 0, h, 0))
    total = parts * heads * rows * keys * chunks
    return pl.pallas_call(
        lambda *refs: forward_kernel(*refs, chunks=chunks, first=first, last=last, bk=bk),
        grid=(parts, heads),
        in_specs=[row_spec] + [key_spec] * chunks + ([] if first else [row_spec, two_spec]),
        out_specs=[row_spec, one_spec, row_spec] if last else [row_spec, two_spec],
        out_shape=[
            jax.ShapeDtypeStruct((parts, width, rows), F),
            jax.ShapeDtypeStruct((parts, heads, 1 if last else 2, rows), F),
        ]
        + ([jax.ShapeDtypeStruct((parts, width, rows), B)] if last else []),
        scratch_shapes=[
            pltpu.VMEM((2 * HD, rows), B),
            pltpu.VMEM((2 * HD, keys * chunks), B),
            pltpu.VMEM((HD + 16, keys * chunks), B),
        ],
        compiler_params=pltpu.CompilerParams(
            vmem_limit_bytes=56 << 20, dimension_semantics=("arbitrary", "arbitrary")
        ),
        cost_estimate=pl.CostEstimate(
            flops=1024 * total, transcendentals=total, bytes_accessed=16 << 20
        ),
        name="attn_forward",
    )(q_t, *kv_list, *(() if first else state))


def backward_kernel(*refs, first, bk, bq):
    q_ref, kv_ref, do_ref, lse_ref, om_ref = refs[:5]
    dq_ref, dkv_ref, qx, kx, dx, vx, dq_acc = refs[-7:]
    rows = q_ref.shape[-1]
    keys = kv_ref.shape[-1]
    scaled = q_ref[0].astype(F) * (score_scale * LOG2E)
    high, rest = split_low(scaled, 2)
    sub = lax.broadcasted_iota(jnp.int32, (16, rows), 0)

    def stacked(value):
        block = jnp.zeros((16, rows), F)
        for j, part in enumerate(split_low(value, 3)):
            block = jnp.where(sub == j, jnp.broadcast_to(part.astype(F), (16, rows)), block)
        return block.astype(B)

    qx[0:HD, :] = high
    qx[HD : 2 * HD, :] = rest
    qx[2 * HD : 2 * HD + 16, :] = stacked(lse_ref[0, 0])
    dx[0:HD, :] = do_ref[0]
    delta = jnp.sum(om_ref[0] * do_ref[0].astype(F), axis=0, keepdims=True)
    dx[HD : HD + 16, :] = stacked(delta)
    kx[0:HD, :] = kv_ref[0, 0]
    kx[HD : 2 * HD, :] = kv_ref[0, 0]
    kx[2 * HD : 2 * HD + 16, :] = jnp.full((16, keys), -1.0, B)
    vx[0:HD, :] = kv_ref[0, 1]
    vx[HD : HD + 16, :] = jnp.full((16, keys), -1.0, B)
    dq_acc[...] = jnp.zeros_like(dq_acc)

    def step(i, carry):
        off = pl.multiple_of(i * bk, bk)
        k_part = kx[:, pl.ds(off, bk)]
        v_part = vx[:, pl.ds(off, bk)]
        dk_part = jnp.zeros((HD, bk), F)
        dv_part = jnp.zeros((HD, bk), F)
        for j in range(0, rows, bq):
            probs = jnp.exp2(dot(qx[:, j : j + bq], k_part, 0, 0))
            prob_grad = dot(dx[:, j : j + bq], v_part, 0, 0)
            score_low = (probs * prob_grad).astype(B)
            prob_low = probs.astype(B)
            dv_part = dv_part + dot(dx[0:HD, j : j + bq], prob_low, 1, 0)
            dk_part = dk_part + dot(q_ref[0, :, j : j + bq], score_low, 1, 0)
            dq_acc[j : j + bq, :] += dot(score_low, k_part[0:HD, :], 1, 1)
        dkv_ref[0, 0, :, pl.ds(off, bk)] = (dk_part * score_scale).astype(B)
        dkv_ref[0, 1, :, pl.ds(off, bk)] = dv_part.astype(B)
        return carry

    lax.fori_loop(0, keys // bk, step, 0)
    total = jnp.transpose(dq_acc[...] * score_scale)
    if not first:
        total = total + refs[5][0]
    dq_ref[0] = total.astype(dq_ref.dtype)


def attention_backward(q_t, kv_t, do_t, lse, om_t, dq_t, last, bk, bq):
    parts, width, rows = q_t.shape
    keys = kv_t.shape[3]
    heads = width // HD
    bk = pick_block(keys, bk)
    bq = pick_block(rows, bq)
    first = dq_t is None
    total = parts * heads * rows * keys
    row_spec = pl.BlockSpec((1, HD, rows), lambda t, h: (t, h, 0))
    stat_spec = pl.BlockSpec((1, 1, 1, rows), lambda t, h: (t, h, 0, 0))
    key_spec = pl.BlockSpec((1, 2, HD, keys), lambda t, h: (t, 0, h, 0))
    return pl.pallas_call(
        lambda *refs: backward_kernel(*refs, first=first, bk=bk, bq=bq),
        grid=(parts, heads),
        in_specs=[row_spec, key_spec, row_spec, stat_spec, row_spec]
        + ([] if first else [row_spec]),
        out_specs=[row_spec, key_spec],
        out_shape=[
            jax.ShapeDtypeStruct((parts, width, rows), B if last else F),
            jax.ShapeDtypeStruct((parts, 2, width, keys), B),
        ],
        scratch_shapes=[
            pltpu.VMEM((2 * HD + 16, rows), B),
            pltpu.VMEM((2 * HD + 16, keys), B),
            pltpu.VMEM((HD + 16, rows), B),
            pltpu.VMEM((HD + 16, keys), B),
            pltpu.VMEM((rows, HD), F),
        ],
        compiler_params=pltpu.CompilerParams(
            vmem_limit_bytes=56 << 20, dimension_semantics=("arbitrary", "arbitrary")
        ),
        cost_estimate=pl.CostEstimate(
            flops=2048 * total, transcendentals=total, bytes_accessed=16 << 20
        ),
        name="attn_backward",
    )(q_t, kv_t, do_t, lse, om_t, *([] if first else [dq_t]))


def gelu_both(u):
    z = jnp.abs(u) * 0.7071067811865476
    t = 1.0 / (1.0 + 0.5 * z)
    series = 0.17087277
    for c in (
        -0.82215223,
        1.48851587,
        -1.13520398,
        0.27886807,
        -0.18628806,
        0.09678418,
        0.37409196,
        1.00002368,
        -1.26551223,
    ):
        series = series * t + c
    bell = jnp.exp(u * u * -0.5)
    tail = (0.5 * t) * bell * jnp.exp(series)
    below = jnp.where(u >= 0, 1.0 - tail, tail)
    return u * below, below + u * (bell * 0.3989422804014327)


def ffn_forward_kernel(y_ref, up_ref, down_ref, bias_ref, act_ref, slope_ref, out_ref, *, br):
    start = (pl.program_id(0) == 0) & (pl.program_id(1) == 0)

    @pl.when(start)
    def _():
        out_ref[...] = jnp.zeros_like(out_ref)

    for r in range(0, y_ref.shape[0], br):
        u = dot(y_ref[r : r + br, :], up_ref[0], 1, 0) + bias_ref[...]
        act, slope = gelu_both(u)
        low = act.astype(B)
        act_ref[r : r + br, :] = low
        slope_ref[r : r + br, :] = slope
        out_ref[r : r + br, :] += dot(low, down_ref[0], 1, 1)


def ffn_backward_kernel(df_ref, up_ref, down_ref, slope_ref, du_ref, sum_ref, out_ref, *, br):
    start = (pl.program_id(0) == 0) & (pl.program_id(1) == 0)

    @pl.when(start)
    def _():
        out_ref[...] = jnp.zeros_like(out_ref)

    total = jnp.zeros(sum_ref.shape, F)
    for r in range(0, df_ref.shape[0], br):
        du = (dot(df_ref[r : r + br, :], down_ref[0], 1, 0) * slope_ref[r : r + br, :]).astype(B)
        du_ref[r : r + br, :] = du
        total = total + jnp.sum(du.astype(F), axis=0, keepdims=True)
        out_ref[r : r + br, :] += dot(du, up_ref[0], 1, 1)
    sum_ref[...] = total


def ffn_specs(rows, width, weights, block, ff_width):
    per = ff_width // block
    up_spec = pl.BlockSpec((1, width, block), lambda t, j: (t, 0, j))
    down_spec = pl.BlockSpec((1, width, block), lambda t, j: (t, 0, per + j))
    row_spec = pl.BlockSpec((rows, width), lambda t, j: (0, 0))
    hidden_spec = pl.BlockSpec((rows, block), lambda t, j: (0, t * per + j))
    vector_spec = pl.BlockSpec((1, block), lambda t, j: (0, t * per + j))
    return (weights.shape[0], per), up_spec, down_spec, row_spec, hidden_spec, vector_spec


FFN_PARAMS = pltpu.CompilerParams(
    vmem_limit_bytes=56 << 20, dimension_semantics=("arbitrary", "arbitrary")
)


def ffn_forward(y_low, weights, bias, block, ff_width):
    rows, width = y_low.shape
    grid, up_spec, down_spec, row_spec, hidden_spec, vector_spec = ffn_specs(
        rows, width, weights, block, ff_width
    )
    hidden = grid[0] * ff_width
    return pl.pallas_call(
        lambda *refs: ffn_forward_kernel(*refs, br=pick_block(rows, 256)),
        grid=grid,
        in_specs=[row_spec, up_spec, down_spec, vector_spec],
        out_specs=[hidden_spec, hidden_spec, row_spec],
        out_shape=[
            jax.ShapeDtypeStruct((rows, hidden), B),
            jax.ShapeDtypeStruct((rows, hidden), F),
            jax.ShapeDtypeStruct((rows, width), F),
        ],
        compiler_params=FFN_PARAMS,
        name="ffn_forward",
    )(y_low, weights, weights, bias)


def ffn_backward(df, weights, slope, block, ff_width):
    rows, width = df.shape
    grid, up_spec, down_spec, row_spec, hidden_spec, vector_spec = ffn_specs(
        rows, width, weights, block, ff_width
    )
    hidden = grid[0] * ff_width
    return pl.pallas_call(
        lambda *refs: ffn_backward_kernel(*refs, br=pick_block(rows, 256)),
        grid=grid,
        in_specs=[row_spec, up_spec, down_spec, hidden_spec],
        out_specs=[hidden_spec, vector_spec, row_spec],
        out_shape=[
            jax.ShapeDtypeStruct((rows, hidden), B),
            jax.ShapeDtypeStruct((1, hidden), F),
            jax.ShapeDtypeStruct((rows, width), F),
        ],
        compiler_params=FFN_PARAMS,
        name="ffn_backward",
    )(df, weights, weights, slope)


def weight_grad_kernel(da_ref, y_ref, df_ref, mixed_ref, du_ref, act_ref, out_ref, *, per):
    j = pl.program_id(1)

    @pl.when(j == 2 * per)
    def _():
        out_ref[0, :, : mixed_ref.shape[1]] = dot(da_ref[...], mixed_ref[0], 0, 1).astype(B)

    @pl.when(j < per)
    def _():
        out_ref[0] = dot(y_ref[...], du_ref[...], 0, 0).astype(B)

    @pl.when((j >= per) & (j < 2 * per))
    def _():
        out_ref[0] = dot(df_ref[...], act_ref[...], 0, 0).astype(B)


def weight_grads(da, y_low, df, mixed_t, du, act, block):
    rows, width = da.shape
    parts, head_width, _ = mixed_t.shape
    per = du.shape[1] // parts // block
    row_spec = pl.BlockSpec((rows, width), lambda t, j: (0, 0))
    return pl.pallas_call(
        lambda *refs: weight_grad_kernel(*refs, per=per),
        grid=(parts, 1 + 2 * per),
        in_specs=[
            row_spec,
            row_spec,
            row_spec,
            pl.BlockSpec((1, head_width, rows), lambda t, j: (t, 0, 0)),
            pl.BlockSpec((rows, block), lambda t, j: (0, t * per + jnp.clip(j, 0, per - 1))),
            pl.BlockSpec((rows, block), lambda t, j: (0, t * per + jnp.clip(j - per, 0, per - 1))),
        ],
        out_specs=pl.BlockSpec((1, width, block), lambda t, j: (t, 0, j)),
        out_shape=jax.ShapeDtypeStruct((parts, width, head_width + 2 * per * block), B),
        compiler_params=FFN_PARAMS,
        name="weight_grads",
    )(da, y_low, df, mixed_t, du, act)


def ring_gather(block):
    count = lax.axis_size("ctx")
    up = [(i, (i + 1) % count) for i in range(count)]
    down = [((i + 1) % count, i) for i in range(count)]
    half = block.shape[0] // 2
    first, second = block[:half], block[half:]
    pieces = []
    for _ in range(1, count):
        first = lax.ppermute(first, "ctx", up)
        second = lax.ppermute(second, "ctx", down)
        pieces.append((first, second))
    return pieces


def ring_return(first, second):
    count = lax.axis_size("ctx")
    up = [(i, (i + 1) % count) for i in range(count)]
    down = [((i + 1) % count, i) for i in range(count)]
    return lax.ppermute(first, "ctx", down), lax.ppermute(second, "ctx", up)


def scatter_sum(blocks, order, extra=None):
    sizes = {axis: lax.axis_size(axis) for axis in WEIGHT_AXES}
    bits = []
    for axis in WEIGHT_AXES:
        bit = sizes[axis] // 2
        while bit:
            bits.append((axis, bit))
            bit //= 2
    left = blocks.reshape((2,) * len(bits) + blocks.shape[2:])
    todo = sorted(
        bits,
        key=lambda one: (one != ("fsdp", 1), order.index(one[0]), -one[1]),
    )
    for axis, bit in todo:
        dim = bits.index((axis, bit))
        bits.remove((axis, bit))
        mine = (lax.axis_index(axis) // bit) % 2
        sent = lax.dynamic_index_in_dim(left, 1 - mine, dim, keepdims=False)
        kept = lax.dynamic_index_in_dim(left, mine, dim, keepdims=False)
        pairs = [(i, i ^ bit) for i in range(sizes[axis])]
        if extra is None:
            got = lax.ppermute(sent, axis, pairs)
        else:
            columns = sent.shape[-1]
            high, low = split_low(extra, 2)
            tail = jnp.concatenate([high, low]).reshape(-1, columns)
            flat = sent.reshape(-1, columns)
            joined = lax.ppermute(jnp.concatenate([flat, tail], axis=0), axis, pairs)
            got = joined[: flat.shape[0]].reshape(sent.shape)
            other = joined[flat.shape[0] :].reshape(2, -1).astype(F)
            extra = (high.astype(F) + low.astype(F)) + (other[0] + other[1])
        total = kept.astype(F) + got.astype(F)
        left = total.astype(B) if bits else total
    return left if extra is None else (left, extra)


def sum_all(vector):
    every = lax.all_gather(vector.reshape(-1, 128), ("fsdp", "ctx", "tp"), axis=0)
    return jnp.sum(every, axis=0).reshape(-1)


def tp_gather(vector):
    size = lax.axis_size("tp")
    own = lax.axis_index("tp")
    out = jnp.zeros((size,) + vector.shape, vector.dtype)
    out = lax.dynamic_update_index_in_dim(out, vector, own, 0)
    for shift in range(1, size):
        got = lax.ppermute(vector, "tp", [(i, (i + shift) % size) for i in range(size)])
        out = lax.dynamic_update_index_in_dim(out, got, (own - shift) % size, 0)
    return out


def tp_exchange(rows):
    size = lax.axis_size("tp")
    own = lax.axis_index("tp")
    seqs, length, width = rows.shape
    split = rows.reshape(seqs, size, length // size, width)
    out = jnp.zeros((size, seqs, length // size, width), rows.dtype)
    kept = lax.dynamic_index_in_dim(split, own, 1, keepdims=False)
    out = lax.dynamic_update_index_in_dim(out, kept, own, 0)
    for shift in range(1, size):
        sent = lax.dynamic_index_in_dim(split, (own + shift) % size, 1, keepdims=False)
        got = lax.ppermute(sent, "tp", [(i, (i + shift) % size) for i in range(size)])
        out = lax.dynamic_update_index_in_dim(out, got, (own - shift) % size, 0)
    return out.reshape(size * seqs, length // size, width)


def norm_forward(hidden, gain, shift):
    center = hidden - jnp.mean(hidden, axis=-1, keepdims=True)
    inv_scale = lax.rsqrt(jnp.mean(center * center, axis=-1, keepdims=True) + epsilon)
    normed = center * inv_scale
    return (normed * gain + shift, normed, inv_scale)


def norm_backward(grad_out, normed, inv_scale, gain):
    grad_norm = grad_out * gain
    return inv_scale * (
        grad_norm
        - jnp.mean(grad_norm, axis=-1, keepdims=True)
        - normed * jnp.mean(grad_norm * normed, axis=-1, keepdims=True)
    )


def layer(
    tokens,
    qkv_weight,
    qv_bias,
    out_weight,
    up_weight,
    up_bias,
    down_weight,
    norm_gains,
    row_biases,
    cotangent,
):
    seq_count, local_len, width = tokens.shape
    tp_count = lax.axis_size("tp")
    own_seqs = seq_count // tp_count
    first_seq = lax.axis_index("tp") * own_seqs
    own_tokens = lax.dynamic_slice_in_dim(tokens, first_seq, own_seqs, 0)
    own_cotangent = lax.dynamic_slice_in_dim(cotangent, first_seq, own_seqs, 0)
    rows = own_seqs * local_len
    x_own = own_tokens.reshape(rows, width)
    shard_rows = qkv_weight.shape[0]
    head_width = qkv_weight.shape[2]
    ff_width = up_weight.shape[1]
    pad = 128 - norm_gains.shape[1] - row_biases.shape[1]

    first_shard = jnp.concatenate(
        [
            qkv_weight.reshape(shard_rows, 3 * head_width),
            norm_gains,
            row_biases,
            jnp.zeros((shard_rows, pad), B),
        ],
        axis=1,
    )
    first_all = lax.all_gather(first_shard, WEIGHT_AXES, axis=0, tiled=True)
    first_all = first_all.reshape(tp_count, width, first_shard.shape[1])
    x_pieces = [ring_gather(own_tokens[s]) for s in range(own_seqs)]
    second_shard = jnp.concatenate([up_weight, down_weight, out_weight], axis=1)
    second_all = lax.all_gather(second_shard, WEIGHT_AXES, axis=0, tiled=True)
    second_all = second_all.reshape(tp_count, width, second_shard.shape[1])
    w_q = first_all[:, :, :head_width]
    w_kv = first_all[:, :, head_width : 3 * head_width]
    rows_all = jnp.transpose(first_all[0, :, 3 * head_width :]).astype(F)
    gain1, gain2 = rows_all[0], rows_all[1]
    out_bias, shift1, down_bias, shift2 = (rows_all[2 + i] for i in range(4))
    w_out = second_all[:, :, 2 * ff_width :]
    bias_all = tp_gather(jnp.concatenate([qv_bias.reshape(-1), up_bias]))
    q_bias = bias_all[:, :head_width].astype(F)
    v_bias = bias_all[:, head_width : 2 * head_width].astype(F)
    u_bias = bias_all[:, 2 * head_width :].astype(F)
    kv_bias = jnp.concatenate([jnp.zeros_like(v_bias), v_bias], axis=1)

    def project(block):
        got = (dot(w_kv, block, 1, 1) + kv_bias[:, :, None]).astype(B)
        return got.reshape(tp_count, 2, head_width, block.shape[0])

    x_chunks = [
        [own_tokens[s]] + [jnp.concatenate(pair, axis=0) for pair in x_pieces[s]]
        for s in range(own_seqs)
    ]
    chunk_count = len(x_chunks[0])
    near = (chunk_count + 1) // 2
    q_t, kv_t, om_t, lse, mixed_s = [], [], [], [], []
    for s in range(own_seqs):
        q_s = (dot(w_q, own_tokens[s], 1, 1) + q_bias[:, :, None]).astype(B)
        kv_s = [project(x_chunks[s][0])]
        kv_s = kv_s + [project(block) for block in x_chunks[s][1:near]]
        if near < chunk_count:
            state = attention_forward(q_s, kv_s, None, False, 2048)
            kv_far = [project(block) for block in x_chunks[s][near:]]
            done = attention_forward(q_s, kv_far, state, True, 2048)
            kv_s = kv_s + kv_far
        else:
            done = attention_forward(q_s, kv_s, None, True, 2048)
        q_t.append(q_s)
        kv_t.append(kv_s)
        om_t.append(done[0])
        lse.append(done[1])
        mixed_s.append(done[2])
    mixed_t = jnp.concatenate(mixed_s, axis=2) if own_seqs > 1 else mixed_s[0]
    attn_part = sum(dot(mixed_t[t], w_out[t], 0, 1) for t in range(tp_count))
    x_float = x_own.astype(F)
    first_out, first_norm, first_scale = norm_forward(
        x_float + attn_part + out_bias, gain1, shift1
    )
    first_low = first_out.astype(B)

    block = ff_width // 2
    act_low, slope, ffn_out = ffn_forward(
        first_low, second_all, u_bias.reshape(1, -1), block, ff_width
    )
    ffn_out = ffn_out + down_bias
    grad_final = own_cotangent.reshape(rows, width).astype(F)
    final_out, final_norm, final_scale = norm_forward(first_out + ffn_out, gain2, shift2)
    output = tp_exchange(final_out.astype(B).reshape(own_seqs, local_len, width))
    gain2_grad = jnp.sum(grad_final * final_norm, axis=0)
    shift2_grad = jnp.sum(grad_final, axis=0)
    grad_second = norm_backward(grad_final, final_norm, final_scale, gain2)
    df = grad_second.astype(B)
    down_bias_grad = jnp.sum(df.astype(F), axis=0)
    inner_low, up_bias_grad, back = ffn_backward(df, second_all, slope, block, ff_width)
    first_grad = grad_second + back
    gain1_grad = jnp.sum(first_grad * first_norm, axis=0)
    shift1_grad = jnp.sum(first_grad, axis=0)
    resid_grad = norm_backward(first_grad, first_norm, first_scale, gain1)
    da = resid_grad.astype(B)
    out_bias_grad = jnp.sum(da.astype(F), axis=0)
    second_grad = weight_grads(da, first_low, df, mixed_t, inner_low, act_low, block)
    do_t = dot(w_out, da, 1, 1).astype(B)
    do_t, second_grad = lax.optimization_barrier((do_t, second_grad))
    second_grad = lax.psum_scatter(
        second_grad.reshape(tp_count * width, second_shard.shape[1]),
        WEIGHT_AXES,
        scatter_dimension=0,
        tiled=True,
    ).astype(F)

    v_bias_grad = jnp.sum(do_t.astype(F), axis=2)
    early = sum_all(
        jnp.concatenate(
            [gain1_grad, gain2_grad, out_bias_grad, shift1_grad, down_bias_grad, shift2_grad]
            + [up_bias_grad.reshape(-1), v_bias_grad.reshape(-1)]
        )
    )
    kv_grad = [0.0] * tp_count
    q_grad = [0.0] * tp_count
    q_bias_grad = 0.0
    own_grads = []
    half = local_len // 2
    for s in range(own_seqs):
        do_s = do_t[:, :, s * local_len : (s + 1) * local_len]
        dq = None
        grads = []
        got = None
        for c in reversed(range(chunk_count)):
            dq, dkv = attention_backward(
                q_t[s], kv_t[s][c], do_s, lse[s], om_t[s], dq, c == 0, 1024, 512
            )
            dkv = dkv.reshape(tp_count, 2 * head_width, dkv.shape[3])
            part = sum(dot(dkv[t], w_kv[t], 0, 1) for t in range(tp_count))
            grads.append((c, dkv))
            if c:
                one, two = part[:half], part[half:]
                if got is not None:
                    one = one + got[0].astype(F)
                    two = two + got[1].astype(F)
                one, two, dq = lax.optimization_barrier((one.astype(B), two.astype(B), dq))
                got = ring_return(one, two)
        dq_low = dq
        for c, dkv in grads:
            kv_grad = [kv_grad[t] + dot(x_chunks[s][c], dkv[t], 0, 1) for t in range(tp_count)]
        q_bias_grad = q_bias_grad + jnp.sum(dq_low.astype(F), axis=2)
        q_grad = [q_grad[t] + dot(own_tokens[s], dq_low[t], 0, 1) for t in range(tp_count)]
        part = part + sum(dot(dq_low[t], w_q[t], 0, 1) for t in range(tp_count))
        if got is not None:
            part = part + jnp.concatenate(got, axis=0).astype(F)
        own_grads.append(part)
    qkv_grad = jnp.stack(
        [jnp.concatenate([q_grad[t], kv_grad[t]], axis=1).astype(B) for t in range(tp_count)]
    )
    qkv_grad = qkv_grad.reshape(tp_count, width // shard_rows, shard_rows, 3 * head_width)
    cut = 2 * head_width - 128
    second_part, q_bias_grad = scatter_sum(
        qkv_grad[..., cut:], ("fsdp", "tp", "ctx"), q_bias_grad.reshape(-1)
    )
    first_part = scatter_sum(qkv_grad[..., :cut], ("tp", "fsdp", "ctx"))
    qkv_grad = jnp.concatenate([first_part, second_part], axis=1)
    tokens_grad = resid_grad.reshape(own_seqs, local_len, width) + jnp.stack(own_grads)
    tokens_out = tp_exchange(tokens_grad.astype(B))

    member = lax.axis_index("fsdp") * lax.axis_size("ctx") + lax.axis_index("ctx")
    own_tp = lax.axis_index("tp")
    six = lax.dynamic_slice_in_dim(
        early[: 6 * width].reshape(6, width), member * shard_rows, shard_rows, 1
    )
    six = jnp.transpose(six)
    up_total = lax.dynamic_slice_in_dim(early, 6 * width + own_tp * ff_width, ff_width, 0)
    v_total = lax.dynamic_slice_in_dim(
        early, 6 * width + tp_count * ff_width + own_tp * head_width, head_width, 0
    )
    q_total = lax.dynamic_slice_in_dim(q_bias_grad, own_tp * head_width, head_width, 0)
    return (
        output,
        tokens_out,
        qkv_grad.reshape(shard_rows, 3, head_width),
        jnp.stack([q_total, v_total]),
        second_grad[:, 2 * ff_width :],
        second_grad[:, :ff_width],
        up_total,
        second_grad[:, ff_width : 2 * ff_width],
        six[:, :2],
        six[:, 2:],
    )


def solution(mesh):
    in_specs = (
        P("fsdp", "ctx", None),
        P(("fsdp", "ctx"), None, "tp"),
        P(None, "tp"),
        P(("fsdp", "ctx"), "tp"),
        P(("fsdp", "ctx"), "tp"),
        P("tp"),
        P(("fsdp", "ctx"), "tp"),
        P(("fsdp", "ctx"), None),
        P(("fsdp", "ctx"), None),
        P("fsdp", "ctx", None),
    )
    out_specs = (
        P("fsdp", ("ctx", "tp"), None),
        P("fsdp", ("ctx", "tp"), None),
        P(("fsdp", "ctx"), None, "tp"),
        P(None, "tp"),
        P(("fsdp", "ctx"), "tp"),
        P(("fsdp", "ctx"), "tp"),
        P("tp"),
        P(("fsdp", "ctx"), "tp"),
        P(("fsdp", "ctx"), None),
        P(("fsdp", "ctx"), None),
    )
    return jax.shard_map(layer, mesh=mesh, in_specs=in_specs, out_specs=out_specs, check_vma=False)
```
